1024 devices in a mesh: lat: 64 (over z, x_lo, core), lev: 16 (over x_hi, y).
Axes of the slice: x: 8 (x_hi: 2, x_lo: 4; x = x_hi * 4 + x_lo), y: 8, z: 8, core: 2. Of those that a mesh axis runs over, the one named last changes fastest.
Arguments:
- state: float32 [128, 16, 512, 256], P('lev', None, 'lat'), may hold values from -6 to 6
- cour_lat: float32 [128, 512, 256], P('lev', 'lat'), may hold values from -0.25 to 0.25
- cour_lev: float32 [128, 512, 256], P('lev', 'lat'), may hold values from -0.25 to 0.25
- cour_lon: float32 [128, 512, 256], P('lev', 'lat'), may hold values from -0.25 to 0.25
- remap_weight: float32 [128, 128], replicated, may hold values from -0.5 to 0.5
- w_in: bfloat16 [2048, 768], replicated, may hold values from -0.125 to 0.125
- w_out: bfloat16 [768, 2048], replicated, may hold values from -0.21875 to 0.21875
- w_rad_in: bfloat16 [512, 1024], replicated, may hold values from -0.25 to 0.25
- radiative_final_weights: bfloat16 [1024, 128], replicated, may hold values from -0.1875 to 0.1875
- day_list: int32 [64, 16, 128], P('lat', 'lev'), may hold values from 0 to 127, as said below
- day_count: int32 [64, 16], P('lat', 'lev'), may hold values from 0 to 8, as said below
Outputs:
- new_state: float32 [128, 16, 512, 256], P('lev', None, 'lat')
The draws below stay inside these ranges and needn't reach their ends.
Inputs may be any that keep to these rules, and one draw needn't show every extreme that they name: Each day_list[b, s] is a permutation of 0 to 127. For every even s, groups s and s + 1 cover the two halves (opposite longitudes) of one latitude row, and day_count[b, s] + day_count[b, s + 1] <= 8; band 0 has a group with exactly 8 blocks.
All inputs are finite; a program needn't handle non-finite values.
Results may differ from the reference program's by a relative error of at most 0.0024.
Values may be sent and summed in bfloat16 or wider, within the bound.
No kernel may reach another device: no remote copies, remote signals or barrier semaphores. Data moves between devices by JAX's collectives and lax.ppermute only.
A program may use at most 64 MiB of HBM per device.

```python
import jax
import jax.numpy as jnp
from jax import lax

L = 128
F = 16
H = 768
RADF = 4
RH = 1024
NLON = 256
COLS_DEV = 128
DB = 16
SUBSTEPS = 1
NLAT = 512
NBAND = 64
NSPLIT = 16
BLK = 8


def draw_day_list(key, part):
    keys = jax.random.split(jax.random.fold_in(key, 11), NBAND * NSPLIT)
    perms = jax.vmap(lambda one_key: jax.random.permutation(one_key, COLS_DEV))(keys)
    return perms.reshape(NBAND, NSPLIT, COLS_DEV).astype(jnp.int32)


def draw_day_count(key, part):
    groups = NLON // COLS_DEV
    half_groups = groups // 2
    key_sun, key_day, key_night = jax.random.split(jax.random.fold_in(key, 23), 3)
    sun_group = jax.random.randint(key_sun, (), 0, groups)
    split_ids = jnp.arange(NSPLIT)
    quarter = split_ids % groups
    is_day = (quarter - sun_group) % groups < half_groups
    partner = jnp.where(quarter < half_groups, split_ids + half_groups, split_ids - half_groups)
    day_value = jax.random.randint(key_day, (NBAND, NSPLIT), BLK - 1, BLK + 1)
    day_value = day_value.at[0].set(BLK)
    night_value = jax.random.randint(key_night, (NBAND, NSPLIT), 0, 2)
    night_value = jnp.minimum(night_value, BLK - day_value[:, partner])
    counts = jnp.where(is_day[None, :], day_value, night_value)
    return counts.astype(jnp.int32)


def level_of(rng, shape, pieces, smallest, top_value):
    factor_of = 1.0
    for position, parts in pieces:
        heights = jax.random.uniform(jax.random.fold_in(jax.random.fold_in(rng, 6), position), (parts,), jnp.float32, smallest / len(pieces), top_value / len(pieces))
        factor_of = factor_of * jnp.repeat(jnp.exp(heights), shape[position] // parts).reshape((-1,) + (1,) * (len(shape) - 1 - position))
    return factor_of


def normal_values(own_key, dims, spread, limit, cuts=(), kind=jnp.bfloat16):
    gain = level_of(own_key, dims, cuts, -0.22, 0.18) if cuts else 1.0
    entries = jax.random.normal(own_key, dims, jnp.float32) * spread * gain
    return jnp.minimum(jnp.maximum(entries, -limit), limit).astype(kind)


def setup_inputs(seed: int = 0) -> dict:
    key_list = jax.random.split(jax.random.key(seed), 12)
    state = normal_values(key_list[0], (L, F, NLAT, NLON), 1.0, 6.0, ((0, 16), (2, 64)), jnp.float32)
    cour_lat = jnp.clip(jax.random.uniform(key_list[1], (L, NLAT, NLON), jnp.float32, -0.25, 0.25) * level_of(key_list[1], (L, NLAT, NLON), ((0, 16), (1, 64)), -0.4, 0.0), -0.25, 0.25)
    cour_lev = jnp.clip(jax.random.uniform(key_list[2], (L, NLAT, NLON), jnp.float32, -0.25, 0.25) * level_of(key_list[2], (L, NLAT, NLON), ((0, 16), (1, 64)), -0.4, 0.0), -0.25, 0.25)
    cour_lon = jnp.clip(jax.random.uniform(key_list[3], (L, NLAT, NLON), jnp.float32, -0.25, 0.25) * level_of(key_list[3], (L, NLAT, NLON), ((0, 16), (1, 64)), -0.4, 0.0), -0.25, 0.25)
    remap_weight = normal_values(key_list[4], (L, L), L ** -0.5, 0.5, (), jnp.float32)
    w_in = normal_values(key_list[5], (L * F, H), (L * F) ** -0.5, 0.125)
    w_out = normal_values(key_list[6], (H, L * F), H ** -0.5, 0.21875)
    w_rad_in = normal_values(key_list[7], (L * RADF, RH), (L * RADF) ** -0.5, 0.25)
    radiative_final_weights = normal_values(key_list[8], (RH, L), RH ** -0.5, 0.1875)
    day_list = draw_day_list(jax.random.fold_in(key_list[11], 71), 0)
    day_count = draw_day_count(jax.random.fold_in(key_list[11], 71), 0)
    return {"state": state, "cour_lat": cour_lat, "cour_lev": cour_lev, "cour_lon": cour_lon, "remap_weight": remap_weight, "w_in": w_in, "w_out": w_out, "w_rad_in": w_rad_in, "radiative_final_weights": radiative_final_weights, "day_list": day_list, "day_count": day_count}


def advance(tracer, north_rate, sinking_speed, east_rate):
    flux_lat = jnp.maximum(north_rate[:, :, :-1], 0.0) * tracer[:, :, :-1] + jnp.minimum(north_rate[:, :, :-1], 0.0) * tracer[:, :, 1:]
    flux_lev = jnp.maximum(sinking_speed[:-1], 0.0) * tracer[:-1] + jnp.minimum(sinking_speed[:-1], 0.0) * tracer[1:]
    flux_lon = jnp.maximum(east_rate, 0.0) * tracer + jnp.minimum(east_rate, 0.0) * jnp.roll(tracer, -1, axis=3)
    div_lat = (flux_lat[:, :, 1:] - flux_lat[:, :, :-1])[1:-1]
    vertical_divergence = (flux_lev[1:] - flux_lev[:-1])[:, :, 1:-1]
    div_lon = (flux_lon - jnp.roll(flux_lon, 1, axis=3))[1:-1, :, 1:-1]
    return tracer[1:-1, :, 1:-1] - div_lat - vertical_divergence - div_lon


def radiate(inputs, w_rad_in, radiative_final_weights):
    levels, nfield = inputs.shape[0], inputs.shape[1]
    rad_hidden = jax.nn.gelu(lax.dot_general(inputs, w_rad_in.reshape(levels, nfield, -1), (((0, 1), (0, 1)), ((), ())), preferred_element_type=jnp.float32)).astype(jnp.bfloat16)
    return lax.dot_general(radiative_final_weights, rad_hidden, (((0,), (1,)), ((), ())), preferred_element_type=jnp.float32)


def physics(remapped, w_in, w_out):
    levels, tracer_fields = remapped.shape[0], remapped.shape[1]
    inputs_bf = remapped.astype(jnp.bfloat16)
    hidden = jax.nn.gelu(lax.dot_general(inputs_bf, w_in.reshape(levels, tracer_fields, -1), (((0, 1), (0, 1)), ((), ())), preferred_element_type=jnp.float32)).astype(jnp.bfloat16)
    tendency = lax.dot_general(w_out.reshape(-1, levels, tracer_fields), hidden, (((0,), (1,)), ((), ())), preferred_element_type=jnp.float32)
    return remapped + tendency


def reference(state, cour_lat, cour_lev, cour_lon, remap_weight, w_in, w_out, w_rad_in, radiative_final_weights, day_list, day_count):
    lat_ids = jnp.arange(NLAT)
    lev_ids = jnp.arange(L)
    masked_lat = cour_lat * (lat_ids < NLAT - 1).astype(jnp.float32)[None, :, None]
    masked_lev = cour_lev * (lev_ids < L - 1).astype(jnp.float32)[:, None, None]

    def pad_rate(values):
        return jnp.pad(values, ((1, 1), (1, 1), (0, 0)))[:, None]

    north_rate = pad_rate(masked_lat)
    sinking_speed = pad_rate(masked_lev)
    east_rate = pad_rate(cour_lon)

    def per_field(values):
        tracer = values[:, None]
        for substep in range(SUBSTEPS):
            padded = jnp.pad(tracer, ((1, 1), (0, 0), (1, 1), (0, 0)))
            tracer = advance(padded, north_rate, sinking_speed, east_rate)
        return tracer[:, 0]

    moved = lax.map(per_field, jnp.moveaxis(state, 1, 0))
    moved = jnp.moveaxis(moved.reshape(F, L, NBAND, NSPLIT * COLS_DEV), 2, 0)
    matrix = jnp.eye(L, dtype=jnp.float32) + remap_weight

    def per_band(packed):
        band_data, band_list, band_count = packed
        columns = band_data.transpose(1, 0, 2)
        remapped = jnp.dot(matrix, columns.reshape(L, -1), precision=lax.Precision.HIGHEST).reshape(columns.shape)
        parameterized_forcing = physics(remapped, w_in, w_out)
        rad_in = parameterized_forcing[:, :RADF].astype(jnp.bfloat16)
        warming_tendency = radiate(rad_in, w_rad_in, radiative_final_weights)
        ranks = jnp.broadcast_to(jnp.arange(COLS_DEV, dtype=jnp.int32)[None, :], (NSPLIT, COLS_DEV))
        coordinate_locations = jnp.zeros((NSPLIT, COLS_DEV), jnp.int32).at[jnp.arange(NSPLIT)[:, None], band_list].set(ranks)
        profile_enabled_flag = (coordinate_locations < (band_count * DB)[:, None]).reshape(-1)
        atmosphere_warmth = parameterized_forcing[:, 0] + jnp.where(profile_enabled_flag[None, :], warming_tendency, 0.0)
        return parameterized_forcing.at[:, 0].set(atmosphere_warmth)

    stepped = lax.map(per_band, (moved, day_list, day_count))
    return jnp.moveaxis(stepped, 0, 2).reshape(L, F, NLAT, NLON)
```

```python
import functools

import jax
import jax.numpy as jnp
from jax import lax
from jax.experimental import pallas as pl
from jax.experimental.pallas import tpu as pltpu
from jax.sharding import PartitionSpec as P

RADF = 4
DB = 16
LANES = 128
BF = jnp.bfloat16
F32 = jnp.float32
VMEM_LIMIT = 24 * 1024 * 1024
SPREAD = 7.0


def call(kernel, name, out_shape, in_specs, scratch=(), flops=0, moved=0, limit=VMEM_LIMIT):
    vmem = pl.BlockSpec(memory_space=pltpu.VMEM)
    return pl.pallas_call(
        kernel,
        name=name,
        out_shape=out_shape,
        in_specs=in_specs,
        out_specs=jax.tree.map(lambda _: vmem, out_shape),
        scratch_shapes=list(scratch),
        compiler_params=pltpu.CompilerParams(vmem_limit_bytes=limit),
        cost_estimate=pl.CostEstimate(flops=flops, bytes_accessed=moved, transcendentals=0),
    )


def pack_kernel(state, cour_lat, cour_lev, lat_up, lat_dn, lev_up, lev_dn):
    nlev, nf, nrow, _ = state.shape
    for level in range(nlev):
        for half in range(nf // 8):
            rows = slice(level * nf + half * 8, level * nf + half * 8 + 8)
            block = state[level, half * 8 : half * 8 + 8]
            lat_up[rows, :] = block[:, nrow - 1, :].astype(BF)
            lat_dn[rows, :] = block[:, 0, :].astype(BF)
    lat_up[nlev * nf :, :] = cour_lat[:, nrow - 1, :].astype(BF)
    for field in range(nf):
        rows = slice(field * nrow, field * nrow + nrow)
        lev_up[rows, :] = state[nlev - 1, field].astype(BF)
        lev_dn[rows, :] = state[0, field].astype(BF)
    lev_up[nf * nrow :, :] = cour_lev[nlev - 1].astype(BF)


def transport_kernel(
    ends, state, cour_lat, cour_lev, cour_lon, from_south, from_north, from_above, from_below,
    moved, sent, south, north, above, below, turned,
):
    nlev, nf, nrow, nlon = state.shape
    south[...] = from_south[...].astype(F32)
    north[...] = from_north[...].astype(F32)
    above[...] = from_above[...].astype(F32)
    below[...] = from_below[...].astype(F32)
    row = lax.broadcasted_iota(jnp.int32, (nrow, nlon), 0)
    first_row, last_row = row == 0, row == nrow - 1
    wide = (nrow, nlon)
    closed_lat = jnp.logical_and(last_row, ends[0] == 1)
    open_lev = jnp.where(ends[1] == 1, 0.0, 1.0).astype(F32)

    def lev_rate(level):
        if level < 0:
            return above[nf * nrow : nf * nrow + nrow, :]
        rate = cour_lev[level]
        return rate * open_lev if level == nlev - 1 else rate

    for level in range(nlev):
        n = jnp.where(closed_lat, 0.0, cour_lat[level])
        halo = jnp.broadcast_to(south[nlev * nf + level : nlev * nf + level + 1, :], wide)
        ns = jnp.where(first_row, halo, pltpu.roll(n, 1, 0))
        d, du = lev_rate(level), lev_rate(level - 1)
        e = cour_lon[level]
        ew = pltpu.roll(e, 1, 1)
        mid = (
            1.0
            - (jnp.maximum(n, 0.0) - jnp.minimum(ns, 0.0))
            - (jnp.maximum(d, 0.0) - jnp.minimum(du, 0.0))
            - (jnp.maximum(e, 0.0) - jnp.minimum(ew, 0.0))
        )
        c_n, c_s = jnp.minimum(n, 0.0), jnp.maximum(ns, 0.0)
        c_d, c_u = jnp.minimum(d, 0.0), jnp.maximum(du, 0.0)
        c_e, c_w = jnp.minimum(e, 0.0), jnp.maximum(ew, 0.0)
        for field in range(nf):
            q = state[level, field]
            at = level * nf + field
            rows = slice(field * nrow, field * nrow + nrow)
            qs = jnp.where(
                first_row, jnp.broadcast_to(south[at : at + 1, :], wide), pltpu.roll(q, 1, 0)
            )
            qn = jnp.where(
                last_row, jnp.broadcast_to(north[at : at + 1, :], wide), pltpu.roll(q, nrow - 1, 0)
            )
            qu = above[rows, :] if level == 0 else state[level - 1, field]
            qd = below[rows, :] if level == nlev - 1 else state[level + 1, field]
            qe = pltpu.roll(q, nlon - 1, 1)
            qw = pltpu.roll(q, 1, 1)
            t = (
                (mid * q + (c_s * qs - c_n * qn))
                + (c_u * qu - c_d * qd)
                + (c_w * qw - c_e * qe)
            )
            moved[level, field] = t
            for half in range(nlon // LANES):
                turned[pl.ds(((field * 2 + half) * nlev + level) * nrow, nrow), :] = t[
                    :, half * LANES : half * LANES + LANES
                ]
    for field in range(nf):
        for half in range(nlon // LANES):
            for r in range(nrow):
                first = (field * 2 + half) * nlev * nrow + r
                tile = turned[pl.ds(first, nlev, stride=nrow), :]
                sent[r * 2 + half, field] = jnp.exp2(tile * SPREAD).astype(BF)


def gelu(x):
    return 0.5 * x * (1.0 + jnp.tanh(0.7978845608028654 * (x + 0.044715 * (x * x * x))))


def column_kernel(
    count, got, remap, w_in, w_out, w_rad, w_heat, day, back,
    whole, split, remapped, extra, hidden, rad_in, rad_hidden, heat,
):
    ngroup, nf, nlev, ncol = got.shape
    levels = ngroup * nlev
    pair = 2 * levels
    w = remap[...]
    high = w.astype(BF)
    low = (w - high.astype(F32)).astype(BF)
    both = jnp.concatenate([high, low], axis=1)
    for field in range(nf):
        code = got[:, field].astype(F32).reshape(levels, ncol)
        t = jnp.log2(code) * (1.0 / SPREAD)
        lanes = slice(field * ncol, field * ncol + ncol)
        th = t.astype(BF)
        whole[:, lanes] = t
        split[:levels, lanes] = th
        split[levels:pair, lanes] = th
        split[pair:, lanes] = (t - th.astype(F32)).astype(BF)
    for two in range(nf // 2):
        lanes = slice(two * 2 * ncol, two * 2 * ncol + 2 * ncol)
        wt = jnp.dot(both, split[:pair, lanes], preferred_element_type=F32) + jnp.dot(
            high, split[pair:, lanes], preferred_element_type=F32
        )
        x = (whole[:, lanes] + wt).astype(BF)
        for k in range(2):
            rows = slice((two * 2 + k) * levels, (two * 2 + k + 1) * levels)
            extra[rows, :] = wt[:, k * ncol : k * ncol + ncol]
            remapped[rows, :] = x[:, k * ncol : k * ncol + ncol]

    nhid = w_in.shape[0]
    chunk = 256

    @pl.loop(0, nhid // chunk)
    def _(i):
        rows = pl.ds(pl.multiple_of(i * chunk, chunk), chunk)
        hidden[rows, :] = gelu(
            jnp.dot(w_in[rows, :], remapped[...], preferred_element_type=F32)
        ).astype(BF)

    @pl.loop(0, nf * levels // pair)
    def _(i):
        rows = pl.ds(pl.multiple_of(i * pair, pair), pair)
        extra[rows, :] = extra[rows, :] + jnp.dot(
            w_out[rows, :], hidden[...], preferred_element_type=F32
        )

    for field in range(RADF):
        rows = slice(field * levels, field * levels + levels)
        lanes = slice(field * ncol, field * ncol + ncol)
        rad_in[rows, :] = (whole[:, lanes] + extra[rows, :]).astype(BF)

    @pl.loop(0, w_rad.shape[0] // chunk)
    def _(i):
        rows = pl.ds(pl.multiple_of(i * chunk, chunk), chunk)
        rad_hidden[rows, :] = gelu(
            jnp.dot(w_rad[rows, :], rad_in[...], preferred_element_type=F32)
        ).astype(BF)

    warm = jnp.dot(w_heat[...], rad_hidden[...], preferred_element_type=F32)
    col = lax.broadcasted_iota(jnp.int32, (ncol, ncol), 0)
    rank = lax.broadcasted_iota(jnp.int32, (ncol, ncol), 1)
    hit = jnp.logical_and(day[...] == col, rank < count[0] * DB)
    lit = lax.dot_general(
        jnp.ones((8, ncol), BF),
        jnp.where(hit, 1.0, 0.0).astype(BF),
        (((1,), (1,)), ((), ())),
        preferred_element_type=F32,
    )
    heat[...] = jnp.where(jnp.broadcast_to(lit[:1, :], warm.shape) > 0.5, warm, 0.0)
    extra[:levels, :] = extra[:levels, :] + heat[...]

    for field in range(nf):
        rows = slice(field * levels, field * levels + levels)
        back[:, field] = extra[rows, :].reshape(ngroup, nlev, ncol).astype(BF)


def finish_kernel(moved, change, out, turned):
    nlev, nf, nrow, nlon = moved.shape
    for field in range(nf):
        for half in range(nlon // LANES):
            for r in range(nrow):
                turned[pl.ds(((field * 2 + half) * nrow + r) * nlev, nlev), :] = change[
                    r * 2 + half, field
                ].astype(F32)
    for field in range(nf):
        for half in range(nlon // LANES):
            lanes = slice(half * LANES, half * LANES + LANES)
            for level in range(nlev):
                first = (field * 2 + half) * nrow * nlev + level
                out[level, field, :, lanes] = (
                    moved[level, field, :, lanes]
                    + turned[pl.ds(first, nrow, stride=nlev), :]
                )


def on_device(
    state, cour_lat, cour_lev, cour_lon, remap_weight, w_in, w_out, w_rad_in,
    radiative_final_weights, day_list, day_count,
):
    nlev, nf, nrow, nlon = state.shape
    nlat_dev, nlev_dev = lax.axis_size("lat"), lax.axis_size("lev")
    levels = nlev * nlev_dev
    ncol = nrow * nlon // nlev_dev
    vmem = pl.BlockSpec(memory_space=pltpu.VMEM)
    smem = pl.BlockSpec(memory_space=pltpu.SMEM)
    shape = jax.ShapeDtypeStruct

    lat_rows, lev_rows = nlev * nf, nf * nrow
    lat_up, lat_dn, lev_up, lev_dn = call(
        pack_kernel,
        "pack",
        (
            shape((lat_rows + nlev, nlon), BF),
            shape((lat_rows, nlon), BF),
            shape((lev_rows + nrow, nlon), BF),
            shape((lev_rows, nlon), BF),
        ),
        [vmem] * 3,
    )(state, cour_lat, cour_lev)
    up_lat = [(i, i + 1) for i in range(nlat_dev - 1)]
    dn_lat = [(i + 1, i) for i in range(nlat_dev - 1)]
    up_lev = [(i, i + 1) for i in range(nlev_dev - 1)]
    dn_lev = [(i + 1, i) for i in range(nlev_dev - 1)]
    from_above = lax.ppermute(lev_up, "lev", up_lev)
    from_below = lax.ppermute(lev_dn, "lev", dn_lev)
    from_south = lax.ppermute(lat_up, "lat", up_lat)
    from_north = lax.ppermute(lat_dn, "lat", dn_lat)

    ends = jnp.stack(
        [lax.axis_index("lat") == nlat_dev - 1, lax.axis_index("lev") == nlev_dev - 1]
    ).astype(jnp.int32)
    groups = 2 * nrow
    moved, sent = call(
        transport_kernel,
        "transport",
        (shape(state.shape, F32), shape((groups, nf, nlev, LANES), BF)),
        [smem] + [vmem] * 8,
        [
            pltpu.VMEM((lat_rows + nlev, nlon), F32),
            pltpu.VMEM((lat_rows, nlon), F32),
            pltpu.VMEM((lev_rows + nrow, nlon), F32),
            pltpu.VMEM((lev_rows, nlon), F32),
            pltpu.VMEM((nf * 2 * nlev * nrow, LANES), F32),
        ],
    )(ends, state, cour_lat, cour_lev, cour_lon, from_south, from_north, from_above, from_below)

    got = lax.all_to_all(sent, "lev", split_axis=0, concat_axis=0, tiled=True)

    nhid, nrad = w_in.shape[1], w_rad_in.shape[1]
    w_in_t = w_in.reshape(levels, nf, nhid).transpose(2, 1, 0).reshape(nhid, nf * levels)
    w_out_t = w_out.reshape(nhid, levels, nf).transpose(2, 1, 0).reshape(nf * levels, nhid)
    w_rad_t = w_rad_in.reshape(levels, RADF, nrad).transpose(2, 1, 0).reshape(nrad, RADF * levels)
    w_heat_t = radiative_final_weights.T
    back = call(
        column_kernel,
        "columns",
        shape(got.shape, BF),
        [smem] + [vmem] * 7,
        [
            pltpu.VMEM((levels, nf * ncol), F32),
            pltpu.VMEM((3 * levels, nf * ncol), BF),
            pltpu.VMEM((nf * levels, ncol), BF),
            pltpu.VMEM((nf * levels, ncol), F32),
            pltpu.VMEM((nhid, ncol), BF),
            pltpu.VMEM((RADF * levels, ncol), BF),
            pltpu.VMEM((nrad, ncol), BF),
            pltpu.VMEM((levels, ncol), F32),
        ],
    )(
        day_count.reshape(1), got, remap_weight, w_in_t, w_out_t, w_rad_t, w_heat_t,
        day_list.reshape(1, -1),
    )

    change = lax.all_to_all(back, "lev", split_axis=0, concat_axis=0, tiled=True)
    return call(
        finish_kernel,
        "finish",
        shape(state.shape, F32),
        [vmem] * 2,
        [pltpu.VMEM((nf * 2 * nlev * nrow, LANES), F32)],
    )(moved, change)


def solution(mesh):
    placed = (
        P("lev", None, "lat", None),
        P("lev", "lat", None),
        P("lev", "lat", None),
        P("lev", "lat", None),
        P(),
        P(),
        P(),
        P(),
        P(),
        P("lat", "lev", None),
        P("lat", "lev"),
    )
    return jax.shard_map(
        on_device,
        mesh=mesh,
        in_specs=placed,
        out_specs=P("lev", None, "lat", None),
        check_vma=False,
    )
```

```python
import jax
import jax.numpy as jnp
from jax import lax
from jax.experimental import pallas as pl
from jax.experimental.pallas import tpu as pltpu
from jax.sharding import PartitionSpec as P

RADF = 4
DB = 16
LANES = 128
BF = jnp.bfloat16
F32 = jnp.float32
VMEM_LIMIT = 16 << 20
FLIP_FLOPS = 4_000_000_000
SPREAD = 7.0


def call(
    kernel, name, out_shape, in_specs, scratch=(), flops=0, moved=0, limit=VMEM_LIMIT
):
    vmem = pl.BlockSpec(memory_space=pltpu.VMEM)
    return pl.pallas_call(
        kernel,
        name=name,
        out_shape=out_shape,
        in_specs=in_specs,
        out_specs=jax.tree.map(lambda _: vmem, out_shape),
        scratch_shapes=list(scratch),
        compiler_params=pltpu.CompilerParams(vmem_limit_bytes=limit),
        cost_estimate=pl.CostEstimate(flops=flops, bytes_accessed=moved, transcendentals=0),
    )


def in_hbm(array):
    return pltpu.with_memory_space_constraint(array, pltpu.HBM)


def fetch(pairs, sems):
    copies = [
        pltpu.make_async_copy(source, target, sems.at[i])
        for i, (source, target) in enumerate(pairs)
    ]
    for copy in copies:
        copy.start()
    return copies


def pack_kernel(
    state_hbm, lat_hbm, lev_hbm, lat_up, lat_dn, lev_up, lev_dn, state, cour_lat, cour_lev, sems
):
    nlev, nf, nrow, _ = state.shape
    order = [0, nlev - 1] + list(range(1, nlev - 1))
    copies = fetch(
        [(lev_hbm.at[nlev - 1], cour_lev), (lat_hbm, cour_lat)]
        + [(state_hbm.at[level], state.at[level]) for level in order],
        sems,
    )
    copies[0].wait()
    lev_up[nf * nrow :, :] = cour_lev[...].astype(BF)
    copies[1].wait()
    lat_up[nlev * nf :, :] = cour_lat[:, nrow - 1, :].astype(BF)
    for place, level in enumerate(order):
        copies[2 + place].wait()
        rows = slice(level * nf, level * nf + nf)
        block = state[level]
        lat_up[rows, :] = block[:, nrow - 1, :].astype(BF)
        lat_dn[rows, :] = block[:, 0, :].astype(BF)
        if level == 0 or level == nlev - 1:
            target = lev_dn if level == 0 else lev_up
            for field in range(nf):
                target[field * nrow : field * nrow + nrow, :] = block[field].astype(BF)


def interior_kernel(
    ends, state_hbm, lat_hbm, lev_hbm, lon_hbm, part, state, cour_lat, cour_lev, cour_lon, sems
):
    nlev, nf, nrow, nlon = state.shape
    copies = fetch(
        [(lat_hbm, cour_lat), (lev_hbm, cour_lev), (lon_hbm, cour_lon)]
        + [(state_hbm.at[level], state.at[level]) for level in range(nlev)],
        sems,
    )
    for copy in copies[:4]:
        copy.wait()
    row = lax.broadcasted_iota(jnp.int32, (nrow, nlon), 0)
    first_row, last_row = row == 0, row == nrow - 1
    closed_lat = jnp.logical_and(last_row, ends[0] == 1)
    open_lev = jnp.where(ends[1] == 1, 0.0, 1.0).astype(F32)
    for level in range(nlev):
        if level < nlev - 1:
            copies[4 + level].wait()
        n = jnp.where(closed_lat, 0.0, cour_lat[level])
        ns = jnp.where(first_row, 0.0, pltpu.roll(n, 1, 0))
        d = cour_lev[level] * open_lev if level == nlev - 1 else cour_lev[level]
        e = cour_lon[level]
        ew = pltpu.roll(e, 1, 1)
        mid = (
            1.0
            - (jnp.maximum(n, 0.0) - jnp.minimum(ns, 0.0))
            - (jnp.maximum(e, 0.0) - jnp.minimum(ew, 0.0))
            - jnp.maximum(d, 0.0)
        )
        c_n, c_s = jnp.where(last_row, 0.0, jnp.minimum(n, 0.0)), jnp.maximum(ns, 0.0)
        c_e, c_w = jnp.minimum(e, 0.0), jnp.maximum(ew, 0.0)
        c_d = jnp.minimum(d, 0.0)
        if level > 0:
            du = cour_lev[level - 1]
            mid = mid + jnp.minimum(du, 0.0)
            c_u = jnp.maximum(du, 0.0)
        for field in range(nf):
            q = state[level, field]
            t = (
                mid * q
                + (c_s * pltpu.roll(q, 1, 0) - c_n * pltpu.roll(q, nrow - 1, 0))
                + (c_w * pltpu.roll(q, 1, 1) - c_e * pltpu.roll(q, nlon - 1, 1))
            )
            if level > 0:
                t = t + c_u * state[level - 1, field]
            if level < nlev - 1:
                t = t - c_d * state[level + 1, field]
            part[level, field] = t


def edge_kernel(
    part, lat_up, lat_dn, lev_up, lev_dn, from_south, from_north, from_above, from_below,
    moved, sent, south, north, turned,
):
    nlev, nf, nrow, nlon = part.shape
    at = nlev * nf
    south_rate = from_south[at:, :].astype(F32)
    north_rate = lat_up[at:, :].astype(F32)
    for level in range(nlev):
        rows = slice(level * nf, level * nf + nf)
        rate = jnp.broadcast_to(south_rate[level : level + 1], (nf, nlon))
        south[rows, :] = jnp.minimum(rate, 0.0) * lat_dn[rows, :].astype(F32) + jnp.maximum(
            rate, 0.0
        ) * from_south[rows, :].astype(F32)
        rate = jnp.broadcast_to(north_rate[level : level + 1], (nf, nlon))
        north[rows, :] = -jnp.minimum(rate, 0.0) * from_north[rows, :].astype(F32)
    row = lax.broadcasted_iota(jnp.int32, (nrow, nlon), 0)
    first_row, last_row = row == 0, row == nrow - 1
    above_rate = from_above[nf * nrow :, :].astype(F32)
    below_rate = lev_up[nf * nrow :, :].astype(F32)
    u_in, u_out = jnp.maximum(above_rate, 0.0), jnp.minimum(above_rate, 0.0)
    d_in = jnp.minimum(below_rate, 0.0)
    for level in range(nlev):
        for field in range(nf):
            at = level * nf + field
            t = part[level, field] + jnp.where(
                first_row,
                jnp.broadcast_to(south[at : at + 1, :], (nrow, nlon)),
                jnp.where(last_row, jnp.broadcast_to(north[at : at + 1, :], (nrow, nlon)), 0.0),
            )
            rows = slice(field * nrow, field * nrow + nrow)
            if level == 0:
                t = (
                    t
                    + u_out * lev_dn[rows, :].astype(F32)
                    + u_in * from_above[rows, :].astype(F32)
                )
            if level == nlev - 1:
                t = t - d_in * from_below[rows, :].astype(F32)
            moved[level, field] = t
            for half in range(nlon // LANES):
                turned[pl.ds(((level * 2 + half) * nf + field) * nrow, nrow), :] = t[
                    :, half * LANES : half * LANES + LANES
                ]
        for half in range(nlon // LANES):
            for r in range(nrow):
                tile = turned[pl.ds((level * 2 + half) * nf * nrow + r, nf, stride=nrow), :]
                sent[r * 2 + half, level] = jnp.exp2(tile * SPREAD).astype(BF)


def flip_kernel(*refs):
    count = (len(refs) - 1) // 3
    source, target, held = (refs[i * count : i * count + count] for i in range(3))
    copies = fetch(zip(source, held), refs[-1])
    for i in range(count):
        copies[i].wait()

        @pl.loop(0, held[i].shape[0] // 256)
        def _(k, source=held[i], target=target[i]):
            rows = pl.ds(pl.multiple_of(k * 256, 256), 256)
            target[:, rows] = source[rows, :].T


def gelu(x):
    return 0.5 * x * (1.0 + jnp.tanh(0.7978845608028654 * (x + 0.044715 * (x * x * x))))


def column_kernel(
    count, got, remap, in_hbm, out_hbm, rad_hbm, heat_hbm, day, back,
    whole, total, remapped, hidden, rad_part, rad_hidden, w_in, w_out, w_rad, w_heat, sems,
):
    ngroup, nlev, nf, ncol = got.shape
    levels = ngroup * nlev
    copies = fetch(
        [(in_hbm, w_in), (out_hbm, w_out), (rad_hbm, w_rad), (heat_hbm, w_heat)], sems
    )
    w = remap[...]
    high = w.astype(BF)
    low = (w - high.astype(F32)).astype(BF)
    both = jnp.concatenate([high, low], axis=1)
    for group in range(ngroup):
        code = got[group].astype(F32).reshape(nlev * nf, ncol)
        whole[group * nlev * nf : (group + 1) * nlev * nf, :] = jnp.log2(code) * (1.0 / SPREAD)
    for two in range(nf // 2):
        fields = [pl.ds(two * 2 + k, levels, stride=nf) for k in range(2)]
        t = jnp.concatenate([whole[rows, :] for rows in fields], axis=1)
        th = t.astype(BF)
        tl = (t - th.astype(F32)).astype(BF)
        x = t + (
            jnp.dot(both, jnp.concatenate([th, th], axis=0), preferred_element_type=F32)
            + jnp.dot(high, tl, preferred_element_type=F32)
        )
        for k, rows in enumerate(fields):
            total[rows, :] = x[:, k * ncol : k * ncol + ncol]
    chunk = 256
    for i in range(nf * levels // chunk):
        rows = slice(i * chunk, i * chunk + chunk)
        remapped[rows, :] = total[rows, :].astype(BF)

    copies[0].wait()

    @pl.loop(0, w_in.shape[0] // chunk)
    def _(i):
        rows = pl.ds(pl.multiple_of(i * chunk, chunk), chunk)
        hidden[rows, :] = gelu(
            jnp.dot(w_in[rows, :], remapped[...], preferred_element_type=F32)
        ).astype(BF)

    copies[1].wait()

    @pl.loop(0, nf * levels // chunk)
    def _(i):
        rows = pl.ds(pl.multiple_of(i * chunk, chunk), chunk)
        total[rows, :] = total[rows, :] + jnp.dot(
            w_out[rows, :], hidden[...], preferred_element_type=F32
        )

    for field in range(RADF):
        rad_part[pl.ds(field, levels, stride=RADF), :] = total[pl.ds(field, levels, stride=nf), :]
    rad_in = rad_part[...].astype(BF)
    copies[2].wait()
    copies[3].wait()

    for i in range(w_rad.shape[0] // chunk):
        rows = slice(i * chunk, i * chunk + chunk)
        rad_hidden[rows, :] = gelu(
            jnp.dot(w_rad[rows, :], rad_in, preferred_element_type=F32)
        ).astype(BF)

    warm = jnp.dot(w_heat[...], rad_hidden[...], preferred_element_type=F32)
    col = lax.broadcasted_iota(jnp.int32, (ncol, ncol), 0)
    rank = lax.broadcasted_iota(jnp.int32, (ncol, ncol), 1)
    hit = jnp.logical_and(day[...] == col, rank < count[0] * DB)
    lit = lax.dot_general(
        jnp.ones((8, ncol), BF),
        jnp.where(hit, 1.0, 0.0).astype(BF),
        (((1,), (1,)), ((), ())),
        preferred_element_type=F32,
    )
    first = pl.ds(0, levels, stride=nf)
    total[first, :] = total[first, :] + jnp.where(
        jnp.broadcast_to(lit[:1, :], warm.shape) > 0.5, warm, 0.0
    )
    for group in range(ngroup):
        rows = slice(group * nlev * nf, (group + 1) * nlev * nf)
        back[group] = (total[rows, :] - whole[rows, :]).astype(BF).reshape(nlev, nf, ncol)


def finish_kernel(moved, change, out, turned):
    nlev, nf, nrow, nlon = moved.shape
    for level in range(nlev):
        for half in range(nlon // LANES):
            base = (level * 2 + half) * nrow * nf
            for r in range(nrow):
                turned[pl.ds(base + r * nf, nf), :] = change[r * 2 + half, level].astype(F32)
            lanes = slice(half * LANES, half * LANES + LANES)
            for field in range(nf):
                out[level, field, :, lanes] = (
                    moved[level, field, :, lanes] + turned[pl.ds(base + field, nrow, stride=nf), :]
                )


def on_device(
    state, cour_lat, cour_lev, cour_lon, remap_weight, w_in, w_out, w_rad_in,
    radiative_final_weights, day_list, day_count,
):
    nlev, nf, nrow, nlon = state.shape
    nlat_dev, nlev_dev = lax.axis_size("lat"), lax.axis_size("lev")
    levels = nlev * nlev_dev
    ncol = nrow * nlon // nlev_dev
    vmem = pl.BlockSpec(memory_space=pltpu.VMEM)
    smem = pl.BlockSpec(memory_space=pltpu.SMEM)
    hbm = pl.BlockSpec(memory_space=pltpu.HBM)
    shape = jax.ShapeDtypeStruct

    lat_rows, lev_rows = nlev * nf, nf * nrow
    packs = call(
        pack_kernel,
        "pack",
        (
            shape((lat_rows + nlev, nlon), BF),
            shape((lat_rows, nlon), BF),
            shape((lev_rows + nrow, nlon), BF),
            shape((lev_rows, nlon), BF),
        ),
        [hbm] * 3,
        [
            pltpu.VMEM(state.shape, F32),
            pltpu.VMEM(cour_lat.shape, F32),
            pltpu.VMEM(cour_lev.shape[1:], F32),
            pltpu.SemaphoreType.DMA((nlev + 2,)),
        ],
        moved=state.size * 4,
        limit=8 << 20,
    )(*map(in_hbm, (state, cour_lat, cour_lev)))
    lat_up, lat_dn, lev_up, lev_dn = packs
    up_lat = [(i, i + 1) for i in range(nlat_dev - 1)]
    dn_lat = [(i + 1, i) for i in range(nlat_dev - 1)]
    up_lev = [(i, i + 1) for i in range(nlev_dev - 1)]
    dn_lev = [(i + 1, i) for i in range(nlev_dev - 1)]
    from_above = lax.ppermute(lev_up, "lev", up_lev)
    from_below = lax.ppermute(lev_dn, "lev", dn_lev)
    from_south = lax.ppermute(lat_up, "lat", up_lat)
    from_north = lax.ppermute(lat_dn, "lat", dn_lat)

    ends = jnp.stack(
        [lax.axis_index("lat") == nlat_dev - 1, lax.axis_index("lev") == nlev_dev - 1]
    ).astype(jnp.int32)
    part = call(
        interior_kernel,
        "interior",
        shape(state.shape, F32),
        [smem] + [hbm] * 4,
        [pltpu.VMEM(state.shape, F32)]
        + [pltpu.VMEM(cour_lat.shape, F32)] * 3
        + [pltpu.SemaphoreType.DMA((nlev + 3,))],
        flops=state.size * 13,
        moved=state.size * 8,
        limit=8 << 20,
    )(ends, *map(in_hbm, (state, cour_lat, cour_lev, cour_lon)))
    moved, sent = call(
        edge_kernel,
        "edges",
        (shape(state.shape, F32), shape((2 * nrow, nlev, nf, LANES), BF)),
        [vmem] * 9,
        [
            pltpu.VMEM((lat_rows, nlon), F32),
            pltpu.VMEM((lat_rows, nlon), F32),
            pltpu.VMEM((nf * 2 * nlev * nrow, LANES), F32),
        ],
        limit=8 << 20,
    )(part, *packs, from_south, from_north, from_above, from_below)

    got = lax.all_to_all(sent, "lev", split_axis=0, concat_axis=0, tiled=True)

    nhid, nrad = w_in.shape[1], w_rad_in.shape[1]
    weights = (w_in, w_out, w_rad_in, radiative_final_weights)
    flipped = call(
        flip_kernel,
        "flip",
        tuple(shape(w.shape[::-1], BF) for w in weights),
        [hbm] * 4,
        [pltpu.VMEM(w.shape, BF) for w in weights] + [pltpu.SemaphoreType.DMA((4,))],
        flops=FLIP_FLOPS,
        moved=2 * sum(w.size * 2 for w in weights),
        limit=16 << 20,
    )(*map(in_hbm, weights))
    back = call(
        column_kernel,
        "columns",
        shape(got.shape, BF),
        [smem, vmem, vmem, hbm, hbm, hbm, hbm, vmem],
        [
            pltpu.VMEM((nf * levels, ncol), F32),
            pltpu.VMEM((nf * levels, ncol), F32),
            pltpu.VMEM((nf * levels, ncol), BF),
            pltpu.VMEM((nhid, ncol), BF),
            pltpu.VMEM((RADF * levels, ncol), F32),
            pltpu.VMEM((nrad, ncol), BF),
        ]
        + [pltpu.VMEM(w.shape[::-1], BF) for w in weights]
        + [pltpu.SemaphoreType.DMA((4,))],
        limit=20 << 20,
    )(day_count.reshape(1), got, remap_weight, *map(in_hbm, flipped), day_list.reshape(1, -1))

    change = lax.all_to_all(back, "lev", split_axis=0, concat_axis=0, tiled=True)
    return call(
        finish_kernel,
        "finish",
        shape(state.shape, F32),
        [vmem] * 2,
        [pltpu.VMEM((nf * 2 * nlev * nrow, LANES), F32)],
        limit=8 << 20,
    )(moved, change)


def solution(mesh):
    placed = (
        P("lev", None, "lat", None),
        P("lev", "lat", None),
        P("lev", "lat", None),
        P("lev", "lat", None),
        P(),
        P(),
        P(),
        P(),
        P(),
        P("lat", "lev", None),
        P("lat", "lev"),
    )
    return jax.shard_map(
        on_device,
        mesh=mesh,
        in_specs=placed,
        out_specs=P("lev", None, "lat", None),
        check_vma=False,
    )
```

```python
import jax
import jax.numpy as jnp
from jax import lax
from jax.experimental import pallas as pl
from jax.experimental.pallas import tpu as pltpu
from jax.sharding import PartitionSpec as P

RADF = 4
DB = 16
LANES = 128
BLOCK = 256
BF = jnp.bfloat16
F32 = jnp.float32
VMEM_LIMIT = 16 << 20
FLIP_FLOPS = 4_000_000_000
SPREAD = 7.0


def call(
    kernel, name, out_shape, in_specs, scratch=(), flops=0, moved=0, limit=VMEM_LIMIT, out_specs=None
):
    vmem = pl.BlockSpec(memory_space=pltpu.VMEM)
    return pl.pallas_call(
        kernel,
        name=name,
        out_shape=out_shape,
        in_specs=in_specs,
        out_specs=out_specs or jax.tree.map(lambda _: vmem, out_shape),
        scratch_shapes=list(scratch),
        compiler_params=pltpu.CompilerParams(vmem_limit_bytes=limit),
        cost_estimate=pl.CostEstimate(flops=flops, bytes_accessed=moved, transcendentals=0),
    )


def in_hbm(array):
    return pltpu.with_memory_space_constraint(array, pltpu.HBM)


def fetch(pairs, sems):
    copies = [
        pltpu.make_async_copy(source, target, sems.at[i])
        for i, (source, target) in enumerate(pairs)
    ]
    for copy in copies:
        copy.start()
    return copies


def pack_kernel(
    ends, state_hbm, lat_hbm, lev_hbm, lat_pair, lat_other, lev_pair, lev_other,
    state, cour_lat, cour_lev, both, sems,
):
    nlev, nf, nrow, _ = state.shape
    order = [0, nlev - 1] + list(range(1, nlev - 1))
    copies = fetch(
        [(lev_hbm.at[nlev - 1], cour_lev), (lat_hbm, cour_lat)]
        + [(state_hbm.at[level], state.at[level]) for level in order],
        sems,
    )
    copies[0].wait()
    lev_pair[nf * nrow :, :] = cour_lev[...].astype(BF)
    lev_other[nf * nrow :, :] = cour_lev[...].astype(BF)
    copies[1].wait()
    rates = cour_lat[:, nrow - 1, :].astype(BF)
    lat_pair[nlev * nf :, :] = rates
    lat_other[nlev * nf :, :] = rates
    copies[2].wait()
    copies[3].wait()
    odd = ends[3]
    for field in range(nf):
        rows = slice(field * nrow, field * nrow + nrow)
        lev_pair[rows, :] = state[(1 - odd) * (nlev - 1), field].astype(BF)
        lev_other[rows, :] = state[odd * (nlev - 1), field].astype(BF)
    for place, level in enumerate(order):
        if place > 1:
            copies[2 + place].wait()
        rows = slice(level * nf, level * nf + nf)
        block = state[level]
        both[0, rows, :] = block[:, nrow - 1, :].astype(BF)
        both[1, rows, :] = block[:, 0, :].astype(BF)
    lat_pair[: nlev * nf, :] = both[ends[2]]
    lat_other[: nlev * nf, :] = both[1 - ends[2]]


def interior_kernel(
    ends, state_hbm, lat_hbm, lev_hbm, lon_hbm, part, state, cour_lat, cour_lev, cour_lon, sems
):
    nlev, nf, nrow, nlon = state.shape
    copies = fetch(
        [(lat_hbm, cour_lat), (lev_hbm, cour_lev), (lon_hbm, cour_lon)]
        + [(state_hbm.at[level], state.at[level]) for level in range(nlev)],
        sems,
    )
    for copy in copies[:4]:
        copy.wait()
    row = lax.broadcasted_iota(jnp.int32, (nrow, nlon), 0)
    first_row, last_row = row == 0, row == nrow - 1
    closed_lat = jnp.logical_and(last_row, ends[0] == 1)
    open_lev = jnp.where(ends[1] == 1, 0.0, 1.0).astype(F32)
    for level in range(nlev):
        if level < nlev - 1:
            copies[4 + level].wait()
        n = jnp.where(closed_lat, 0.0, cour_lat[level])
        ns = jnp.where(first_row, 0.0, pltpu.roll(n, 1, 0))
        d = cour_lev[level] * open_lev if level == nlev - 1 else cour_lev[level]
        e = cour_lon[level]
        ew = pltpu.roll(e, 1, 1)
        mid = (
            1.0
            - (jnp.maximum(n, 0.0) - jnp.minimum(ns, 0.0))
            - (jnp.maximum(e, 0.0) - jnp.minimum(ew, 0.0))
            - jnp.maximum(d, 0.0)
        )
        c_n, c_s = jnp.where(last_row, 0.0, jnp.minimum(n, 0.0)), jnp.maximum(ns, 0.0)
        c_e, c_w = jnp.minimum(e, 0.0), jnp.maximum(ew, 0.0)
        c_d = jnp.minimum(d, 0.0)
        if level > 0:
            du = cour_lev[level - 1]
            mid = mid + jnp.minimum(du, 0.0)
            c_u = jnp.maximum(du, 0.0)
        for field in range(nf):
            q = state[level, field]
            t = (
                mid * q
                + (c_s * pltpu.roll(q, 1, 0) - c_n * pltpu.roll(q, nrow - 1, 0))
                + (c_w * pltpu.roll(q, 1, 1) - c_e * pltpu.roll(q, nlon - 1, 1))
            )
            if level > 0:
                t = t + c_u * state[level - 1, field]
            if level < nlev - 1:
                t = t - c_d * state[level + 1, field]
            part[level, field] = t


def edge_kernel(
    ends, part, lat_pair, lat_other, lev_pair, lev_other,
    from_lat_pair, from_lat_other, from_lev_pair, from_lev_other,
    moved, sent, south, north, turned,
):
    nlev, nf, nrow, nlon = part.shape
    lat_odd, lev_odd = ends[2] == 1, ends[3] == 1

    def pick(odd, rows, if_odd, if_even):
        return jnp.where(odd, if_odd[rows, :].astype(F32), if_even[rows, :].astype(F32))

    tail = slice(nlev * nf, nlev * nf + nlev)
    south_rate = pick(lat_odd, tail, from_lat_pair, from_lat_other)
    north_rate = lat_pair[tail, :].astype(F32)
    for level in range(nlev):
        rows = slice(level * nf, level * nf + nf)
        rate = jnp.broadcast_to(south_rate[level : level + 1], (nf, nlon))
        south[rows, :] = jnp.minimum(rate, 0.0) * pick(
            lat_odd, rows, lat_pair, lat_other
        ) + jnp.maximum(rate, 0.0) * pick(lat_odd, rows, from_lat_pair, from_lat_other)
        rate = jnp.broadcast_to(north_rate[level : level + 1], (nf, nlon))
        north[rows, :] = -jnp.minimum(rate, 0.0) * pick(
            lat_odd, rows, from_lat_other, from_lat_pair
        )
    row = lax.broadcasted_iota(jnp.int32, (nrow, nlon), 0)
    first_row, last_row = row == 0, row == nrow - 1
    tail = slice(nf * nrow, nf * nrow + nrow)
    above_rate = pick(lev_odd, tail, from_lev_pair, from_lev_other)
    below_rate = lev_pair[tail, :].astype(F32)
    u_in, u_out = jnp.maximum(above_rate, 0.0), jnp.minimum(above_rate, 0.0)
    d_in = jnp.minimum(below_rate, 0.0)
    for field in range(nf):
        for level in range(nlev):
            at = level * nf + field
            t = part[level, field] + jnp.where(
                first_row,
                jnp.broadcast_to(south[at : at + 1, :], (nrow, nlon)),
                jnp.where(last_row, jnp.broadcast_to(north[at : at + 1, :], (nrow, nlon)), 0.0),
            )
            rows = slice(field * nrow, field * nrow + nrow)
            if level == 0:
                t = (
                    t
                    + u_out * pick(lev_odd, rows, lev_pair, lev_other)
                    + u_in * pick(lev_odd, rows, from_lev_pair, from_lev_other)
                )
            if level == nlev - 1:
                t = t - d_in * pick(lev_odd, rows, from_lev_other, from_lev_pair)
            moved[level, field] = t
            for half in range(nlon // LANES):
                turned[pl.ds(((field * 2 + half) * nlev + level) * nrow, nrow), :] = t[
                    :, half * LANES : half * LANES + LANES
                ]
        for half in range(nlon // LANES):
            for r in range(nrow):
                tile = turned[pl.ds((field * 2 + half) * nlev * nrow + r, nlev, stride=nrow), :]
                sent[r * 2 + half, field] = jnp.exp2(tile * SPREAD).astype(BF)


def swap_rows(rows, inner):
    to = lax.broadcasted_iota(jnp.int32, (rows, rows), 0)
    source = lax.broadcasted_iota(jnp.int32, (rows, rows), 1)
    outer = rows // inner
    wanted = lax.rem(to, outer) * inner + lax.div(to, outer)
    return jnp.where(source == wanted, 1.0, 0.0).astype(BF)


def flip_kernel(
    in_hbm, out_hbm, rad_hbm, heat_hbm, in_t_hbm, out_t_hbm, rad_t_hbm, heat_t_hbm,
    w_in, w_out, w_rad, w_heat, in_t, out_t, rad_t, heat_t, perm, sems, out_sems,
):
    copies = fetch([(in_hbm, w_in), (out_hbm, w_out), (rad_hbm, w_rad), (heat_hbm, w_heat)], sems)
    perm[...] = swap_rows(BLOCK, BLOCK // 16)
    results = []

    def done(source, target):
        results.append(pltpu.make_async_copy(source, target, out_sems.at[len(results)]))
        results[-1].start()

    copies[0].wait()

    @pl.loop(0, w_in.shape[0] // BLOCK)
    def _(k):
        rows = pl.ds(pl.multiple_of(k * BLOCK, BLOCK), BLOCK)
        in_t[:, rows] = (
            jnp.dot(perm[...], w_in[rows, :], preferred_element_type=F32).astype(BF).T
        )

    done(in_t, in_t_hbm)
    copies[1].wait()

    @pl.loop(0, w_out.shape[1] // BLOCK)
    def _(k):
        rows = pl.ds(pl.multiple_of(k * BLOCK, BLOCK), BLOCK)
        out_t[rows, :] = jnp.dot(
            perm[...], w_out[:, rows].T, preferred_element_type=F32
        ).astype(BF)

    done(out_t, out_t_hbm)
    perm[...] = swap_rows(BLOCK, RADF)
    copies[2].wait()
    for k in range(w_rad.shape[0] // BLOCK):
        rows = slice(k * BLOCK, k * BLOCK + BLOCK)
        rad_t[:, rows] = (
            jnp.dot(perm[...], w_rad[rows, :], preferred_element_type=F32).astype(BF).T
        )
    done(rad_t, rad_t_hbm)
    copies[3].wait()
    heat_t[...] = w_heat[...].T
    done(heat_t, heat_t_hbm)
    for copy in results:
        copy.wait()


def gelu(x):
    return 0.5 * x * (1.0 + jnp.tanh(0.7978845608028654 * (x + 0.044715 * (x * x * x))))


def column_kernel(
    count, got, remap, in_hbm, out_hbm, rad_hbm, heat_hbm, day, back,
    whole, total, remapped, hidden, rad_in, rad_hidden, w_in, w_out, w_rad, w_heat, sems,
):
    copies = fetch(
        [(in_hbm, w_in), (out_hbm, w_out), (rad_hbm, w_rad), (heat_hbm, w_heat)], sems
    )
    ngroup, nf, nlev, ncol = got.shape
    levels = ngroup * nlev
    deep = BLOCK // nf
    w = remap[...]
    high = w.astype(BF)
    low = (w - high.astype(F32)).astype(BF)
    both = jnp.concatenate([high, low], axis=1)
    for two in range(nf // 2):
        ts = []
        for k in range(2):
            field = two * 2 + k
            code = got[:, field].astype(F32).reshape(levels, ncol)
            ts.append(jnp.log2(code) * (1.0 / SPREAD))
            whole[field * levels : field * levels + levels, :] = ts[-1]
        t = jnp.concatenate(ts, axis=1)
        th = t.astype(BF)
        tl = (t - th.astype(F32)).astype(BF)
        x = t + (
            jnp.dot(both, jnp.concatenate([th, th], axis=0), preferred_element_type=F32)
            + jnp.dot(high, tl, preferred_element_type=F32)
        )
        for k in range(2):
            for block in range(levels // deep):
                at = block * BLOCK + (two * 2 + k) * deep
                tile = x[block * deep : block * deep + deep, k * ncol : k * ncol + ncol]
                total[at : at + deep, :] = tile
                remapped[at : at + deep, :] = tile.astype(BF)
    copies[0].wait()
    for i in range(w_in.shape[0] // BLOCK):
        rows = slice(i * BLOCK, i * BLOCK + BLOCK)
        hidden[rows, :] = gelu(
            jnp.dot(w_in[rows, :], remapped[...], preferred_element_type=F32)
        ).astype(BF)
    copies[1].wait()
    blocks_each = levels // deep // (w_rad.shape[1] // BLOCK)
    for i in range(nf * levels // BLOCK):
        rows = slice(i * BLOCK, i * BLOCK + BLOCK)
        total[rows, :] = total[rows, :] + jnp.dot(
            w_out[rows, :], hidden[...], preferred_element_type=F32
        )
        for field in range(RADF):
            at = (i // blocks_each) * BLOCK + (field * blocks_each + i % blocks_each) * deep
            first = i * BLOCK + field * deep
            rad_in[at : at + deep, :] = total[first : first + deep, :].astype(BF)
    copies[2].wait()
    copies[3].wait()
    for i in range(w_rad.shape[0] // BLOCK):
        rows = slice(i * BLOCK, i * BLOCK + BLOCK)
        rad_hidden[rows, :] = gelu(
            jnp.dot(w_rad[rows, :], rad_in[...], preferred_element_type=F32)
        ).astype(BF)
    for field in range(1, nf):
        for group in range(ngroup):
            at = (group * nlev // deep) * BLOCK + field * deep + group * nlev % deep
            own = field * levels + group * nlev
            back[group, field] = (total[at : at + nlev, :] - whole[own : own + nlev, :]).astype(BF)
    warm = jnp.dot(w_heat[...], rad_hidden[...], preferred_element_type=F32)
    col = lax.broadcasted_iota(jnp.int32, (ncol, ncol), 0)
    rank = lax.broadcasted_iota(jnp.int32, (ncol, ncol), 1)
    hit = jnp.logical_and(day[...] == col, rank < count[0] * DB)
    lit = lax.dot_general(
        jnp.ones((8, ncol), BF),
        jnp.where(hit, 1.0, 0.0).astype(BF),
        (((1,), (1,)), ((), ())),
        preferred_element_type=F32,
    )
    warm = jnp.where(jnp.broadcast_to(lit[:1, :], warm.shape) > 0.5, warm, 0.0)
    for group in range(ngroup):
        at = (group * nlev // deep) * BLOCK + group * nlev % deep
        own = group * nlev
        back[group, 0] = (
            total[at : at + nlev, :] - whole[own : own + nlev, :] + warm[own : own + nlev, :]
        ).astype(BF)


def finish_kernel(moved, change, out, turned):
    nlev, nf, nrow, nlon = moved.shape
    for field in range(nf):
        for half in range(nlon // LANES):
            base = (field * 2 + half) * nrow * nlev
            for r in range(nrow):
                turned[pl.ds(base + r * nlev, nlev), :] = change[r * 2 + half, field].astype(F32)
            lanes = slice(half * LANES, half * LANES + LANES)
            for level in range(nlev):
                out[level, field, :, lanes] = (
                    moved[level, field, :, lanes]
                    + turned[pl.ds(base + level, nrow, stride=nlev), :]
                )


def on_device(
    state, cour_lat, cour_lev, cour_lon, remap_weight, w_in, w_out, w_rad_in,
    radiative_final_weights, day_list, day_count,
):
    nlev, nf, nrow, nlon = state.shape
    nlat_dev, nlev_dev = lax.axis_size("lat"), lax.axis_size("lev")
    levels = nlev * nlev_dev
    ncol = nrow * nlon // nlev_dev
    vmem = pl.BlockSpec(memory_space=pltpu.VMEM)
    smem = pl.BlockSpec(memory_space=pltpu.SMEM)
    hbm = pl.BlockSpec(memory_space=pltpu.HBM)
    shape = jax.ShapeDtypeStruct

    lat_rows, lev_rows = nlev * nf, nf * nrow
    lat_at, lev_at = lax.axis_index("lat"), lax.axis_index("lev")
    ends = jnp.stack(
        [lat_at == nlat_dev - 1, lev_at == nlev_dev - 1, lat_at & 1 == 1, lev_at & 1 == 1]
    ).astype(jnp.int32)
    packs = call(
        pack_kernel,
        "pack",
        (shape((lat_rows + nlev, nlon), BF),) * 2 + (shape((lev_rows + nrow, nlon), BF),) * 2,
        [smem] + [hbm] * 3,
        [
            pltpu.VMEM(state.shape, F32),
            pltpu.VMEM(cour_lat.shape, F32),
            pltpu.VMEM(cour_lev.shape[1:], F32),
            pltpu.VMEM((2, lat_rows, nlon), BF),
            pltpu.SemaphoreType.DMA((nlev + 2,)),
        ],
        moved=state.size * 4,
        limit=8 << 20,
    )(ends, *map(in_hbm, (state, cour_lat, cour_lev)))

    def trade(value, axis, count, first):
        pairs = [(i, i + 1) for i in range(first, count - 1, 2)]
        return lax.ppermute(value, axis, pairs + [(j, i) for i, j in pairs])

    halos = [
        trade(packs[0], "lat", nlat_dev, 0),
        trade(packs[1], "lat", nlat_dev, 1),
        trade(packs[2], "lev", nlev_dev, 0),
        trade(packs[3], "lev", nlev_dev, 1),
    ]
    part = call(
        interior_kernel,
        "interior",
        shape(state.shape, F32),
        [smem] + [hbm] * 4,
        [pltpu.VMEM(state.shape, F32)]
        + [pltpu.VMEM(cour_lat.shape, F32)] * 3
        + [pltpu.SemaphoreType.DMA((nlev + 3,))],
        flops=state.size * 13,
        moved=state.size * 8,
        limit=8 << 20,
    )(ends, *map(in_hbm, (state, cour_lat, cour_lev, cour_lon)))
    moved, sent = call(
        edge_kernel,
        "edges",
        (shape(state.shape, F32), shape((2 * nrow, nf, nlev, LANES), BF)),
        [smem] + [vmem] * 9,
        [
            pltpu.VMEM((lat_rows, nlon), F32),
            pltpu.VMEM((lat_rows, nlon), F32),
            pltpu.VMEM((nf * 2 * nlev * nrow, LANES), F32),
        ],
        limit=8 << 20,
    )(ends, part, *packs, *halos)

    got = lax.all_to_all(sent, "lev", split_axis=0, concat_axis=0, tiled=True)

    nhid, nrad = w_in.shape[1], w_rad_in.shape[1]
    weights = (w_in, w_out, w_rad_in, radiative_final_weights)
    flipped = call(
        flip_kernel,
        "flip",
        tuple(pltpu.HBM(w.shape[::-1], BF) for w in weights),
        [hbm] * 4,
        [pltpu.VMEM(w.shape, BF) for w in weights]
        + [pltpu.VMEM(w.shape[::-1], BF) for w in weights]
        + [pltpu.VMEM((BLOCK, BLOCK), BF)]
        + [pltpu.SemaphoreType.DMA((4,))] * 2,
        flops=FLIP_FLOPS,
        moved=2 * sum(w.size * 2 for w in weights),
        limit=20 << 20,
        out_specs=(hbm,) * 4,
    )(*map(in_hbm, weights))
    back = call(
        column_kernel,
        "columns",
        shape(got.shape, BF),
        [smem, vmem, vmem, hbm, hbm, hbm, hbm, vmem],
        [
            pltpu.VMEM((nf * levels, ncol), F32),
            pltpu.VMEM((nf * levels, ncol), F32),
            pltpu.VMEM((nf * levels, ncol), BF),
            pltpu.VMEM((nhid, ncol), BF),
            pltpu.VMEM((RADF * levels, ncol), BF),
            pltpu.VMEM((nrad, ncol), BF),
        ]
        + [pltpu.VMEM(w.shape[::-1], BF) for w in weights]
        + [pltpu.SemaphoreType.DMA((4,))],
        limit=20 << 20,
    )(day_count.reshape(1), got, remap_weight, *map(in_hbm, flipped), day_list.reshape(1, -1))

    change = lax.all_to_all(back, "lev", split_axis=0, concat_axis=0, tiled=True)
    return call(
        finish_kernel,
        "finish",
        shape(state.shape, F32),
        [vmem] * 2,
        [pltpu.VMEM((nf * 2 * nlev * nrow, LANES), F32)],
        limit=8 << 20,
    )(moved, change)


def solution(mesh):
    placed = (
        P("lev", None, "lat", None),
        P("lev", "lat", None),
        P("lev", "lat", None),
        P("lev", "lat", None),
        P(),
        P(),
        P(),
        P(),
        P(),
        P("lat", "lev", None),
        P("lat", "lev"),
    )
    return jax.shard_map(
        on_device,
        mesh=mesh,
        in_specs=placed,
        out_specs=P("lev", None, "lat", None),
        check_vma=False,
    )
```

```python
import jax
import jax.numpy as jnp
from jax import lax
from jax.experimental import pallas as pl
from jax.experimental.pallas import tpu as pltpu
from jax.sharding import PartitionSpec as P

RADF = 4
DB = 16
LANES = 128
BLOCK = 256
SOME = 4
BF = jnp.bfloat16
F32 = jnp.float32
VMEM_LIMIT = 16 << 20
FLIP_FLOPS = 4_000_000_000
SPREAD = 7.0


def call(
    kernel, name, out_shape, in_specs, scratch=(), flops=0, moved=0, limit=VMEM_LIMIT, out_specs=None
):
    vmem = pl.BlockSpec(memory_space=pltpu.VMEM)
    return pl.pallas_call(
        kernel,
        name=name,
        out_shape=out_shape,
        in_specs=in_specs,
        out_specs=out_specs or jax.tree.map(lambda _: vmem, out_shape),
        scratch_shapes=list(scratch),
        compiler_params=pltpu.CompilerParams(vmem_limit_bytes=limit),
        cost_estimate=pl.CostEstimate(flops=flops, bytes_accessed=moved, transcendentals=0),
    )


def in_hbm(array):
    return pltpu.with_memory_space_constraint(array, pltpu.HBM)


def fetch(pairs, sems):
    copies = [
        pltpu.make_async_copy(source, target, sems.at[i])
        for i, (source, target) in enumerate(pairs)
    ]
    for copy in copies:
        copy.start()
    return copies


def pack_kernel(
    state_hbm, lat_hbm, lev_hbm, lon_hbm, lat_pair, lat_other, lev_pair, lev_other,
    state, cour_lat, cour_lev, cour_lon, both, sems,
):
    nlev, nf, nrow, _ = state.shape
    order = [0, nlev - 1] + list(range(1, nlev - 1))
    copies = fetch(
        [(lev_hbm, cour_lev), (lat_hbm, cour_lat)]
        + [(state_hbm.at[level], state.at[level]) for level in order]
        + [(lon_hbm, cour_lon)],
        sems,
    )
    copies[0].wait()
    lev_pair[nf * nrow :, :] = cour_lev[nlev - 1].astype(BF)
    lev_other[nf * nrow :, :] = cour_lev[nlev - 1].astype(BF)
    copies[1].wait()
    rates = cour_lat[:, nrow - 1, :].astype(BF)
    lat_pair[nlev * nf :, :] = rates
    lat_other[nlev * nf :, :] = rates
    copies[2].wait()
    copies[3].wait()
    odd = lax.axis_index("lev") & 1
    lat_odd = lax.axis_index("lat") & 1
    for field in range(nf):
        rows = slice(field * nrow, field * nrow + nrow)
        lev_pair[rows, :] = state[(1 - odd) * (nlev - 1), field].astype(BF)
        lev_other[rows, :] = state[odd * (nlev - 1), field].astype(BF)
    for place, level in enumerate(order):
        if place > 1:
            copies[2 + place].wait()
        rows = slice(level * nf, level * nf + nf)
        block = state[level]
        both[0, rows, :] = block[:, nrow - 1, :].astype(BF)
        both[1, rows, :] = block[:, 0, :].astype(BF)
    lat_pair[: nlev * nf, :] = both[lat_odd]
    lat_other[: nlev * nf, :] = both[1 - lat_odd]
    copies[-1].wait()


def interior_kernel(state, cour_lat, cour_lev, cour_lon, part):
    nlev, nf, nrow, nlon = state.shape
    last_lat = lax.axis_index("lat") == lax.axis_size("lat") - 1
    last_lev = lax.axis_index("lev") == lax.axis_size("lev") - 1
    row = lax.broadcasted_iota(jnp.int32, (nrow, nlon), 0)
    first_row, last_row = row == 0, row == nrow - 1
    closed_lat = jnp.logical_and(last_row, last_lat)
    open_lev = jnp.where(last_lev, 0.0, 1.0).astype(F32)
    for level in range(nlev):
        n = jnp.where(closed_lat, 0.0, cour_lat[level])
        ns = jnp.where(first_row, 0.0, pltpu.roll(n, 1, 0))
        d = cour_lev[level] * open_lev if level == nlev - 1 else cour_lev[level]
        e = cour_lon[level]
        ew = pltpu.roll(e, 1, 1)
        mid = (
            1.0
            - (jnp.maximum(n, 0.0) - jnp.minimum(ns, 0.0))
            - (jnp.maximum(e, 0.0) - jnp.minimum(ew, 0.0))
            - jnp.maximum(d, 0.0)
        )
        c_n, c_s = jnp.where(last_row, 0.0, jnp.minimum(n, 0.0)), jnp.maximum(ns, 0.0)
        c_e, c_w = jnp.minimum(e, 0.0), jnp.maximum(ew, 0.0)
        c_d = jnp.minimum(d, 0.0)
        if level > 0:
            du = cour_lev[level - 1]
            mid = mid + jnp.minimum(du, 0.0)
            c_u = jnp.maximum(du, 0.0)
        for field in range(nf):
            q = state[level, field]
            t = (
                mid * q
                + (c_s * pltpu.roll(q, 1, 0) - c_n * pltpu.roll(q, nrow - 1, 0))
                + (c_w * pltpu.roll(q, 1, 1) - c_e * pltpu.roll(q, nlon - 1, 1))
            )
            if level > 0:
                t = t + c_u * state[level - 1, field]
            if level < nlev - 1:
                t = t - c_d * state[level + 1, field]
            part[level, field] = t


def edge_kernel(
    part, lat_pair, lat_other, lev_pair, lev_other,
    from_lat_pair, from_lat_other, from_lev_pair, from_lev_other,
    moved, sent_hbm, south, north, turned, sent, sems,
):
    nlev, nf, nrow, nlon = part.shape
    lat_odd, lev_odd = lax.axis_index("lat") & 1 == 1, lax.axis_index("lev") & 1 == 1

    def pick(odd, rows, if_odd, if_even):
        return jnp.where(odd, if_odd[rows, :].astype(F32), if_even[rows, :].astype(F32))

    tail = slice(nlev * nf, nlev * nf + nlev)
    south_rate = pick(lat_odd, tail, from_lat_pair, from_lat_other)
    north_rate = lat_pair[tail, :].astype(F32)
    for level in range(nlev):
        rows = slice(level * nf, level * nf + nf)
        rate = jnp.broadcast_to(south_rate[level : level + 1], (nf, nlon))
        south[rows, :] = jnp.minimum(rate, 0.0) * pick(
            lat_odd, rows, lat_pair, lat_other
        ) + jnp.maximum(rate, 0.0) * pick(lat_odd, rows, from_lat_pair, from_lat_other)
        rate = jnp.broadcast_to(north_rate[level : level + 1], (nf, nlon))
        north[rows, :] = -jnp.minimum(rate, 0.0) * pick(
            lat_odd, rows, from_lat_other, from_lat_pair
        )
    row = lax.broadcasted_iota(jnp.int32, (nrow, nlon), 0)
    first_row, last_row = row == 0, row == nrow - 1
    tail = slice(nf * nrow, nf * nrow + nrow)
    above_rate = pick(lev_odd, tail, from_lev_pair, from_lev_other)
    below_rate = lev_pair[tail, :].astype(F32)
    u_in, u_out = jnp.maximum(above_rate, 0.0), jnp.minimum(above_rate, 0.0)
    d_in = jnp.minimum(below_rate, 0.0)
    copies = []
    for field in range(nf):
        for level in range(nlev):
            at = level * nf + field
            t = part[level, field] + jnp.where(
                first_row,
                jnp.broadcast_to(south[at : at + 1, :], (nrow, nlon)),
                jnp.where(last_row, jnp.broadcast_to(north[at : at + 1, :], (nrow, nlon)), 0.0),
            )
            rows = slice(field * nrow, field * nrow + nrow)
            if level == 0:
                t = (
                    t
                    + u_out * pick(lev_odd, rows, lev_pair, lev_other)
                    + u_in * pick(lev_odd, rows, from_lev_pair, from_lev_other)
                )
            if level == nlev - 1:
                t = t - d_in * pick(lev_odd, rows, from_lev_other, from_lev_pair)
            moved[level, field] = t
            for half in range(nlon // LANES):
                turned[pl.ds(((field * 2 + half) * nlev + level) * nrow, nrow), :] = t[
                    :, half * LANES : half * LANES + LANES
                ]
        for half in range(nlon // LANES):
            for r in range(nrow):
                tile = turned[pl.ds((field * 2 + half) * nlev * nrow + r, nlev, stride=nrow), :]
                sent[r * 2 + half, field] = jnp.exp2(tile * SPREAD).astype(BF)
        if (field + 1) % SOME == 0:
            put = slice(field + 1 - SOME, field + 1)
            copies += fetch([(sent.at[:, put], sent_hbm.at[:, put])], sems.at[field // SOME])
    for copy in copies:
        copy.wait()


def swap_rows(rows, inner):
    to = lax.broadcasted_iota(jnp.int32, (rows, rows), 0)
    source = lax.broadcasted_iota(jnp.int32, (rows, rows), 1)
    outer = rows // inner
    wanted = lax.rem(to, outer) * inner + lax.div(to, outer)
    return jnp.where(source == wanted, 1.0, 0.0).astype(BF)


def flip_kernel(
    in_hbm, out_hbm, rad_hbm, heat_hbm, in_t_hbm, out_t_hbm, rad_t_hbm, heat_t_hbm,
    w_in, w_out, w_rad, w_heat, in_t, out_t, rad_t, heat_t, perm, sems, out_sems,
):
    copies = fetch([(in_hbm, w_in), (out_hbm, w_out), (rad_hbm, w_rad), (heat_hbm, w_heat)], sems)
    perm[...] = swap_rows(BLOCK, BLOCK // 16)
    results = []

    def done(source, target):
        results.append(pltpu.make_async_copy(source, target, out_sems.at[len(results)]))
        results[-1].start()

    copies[0].wait()

    @pl.loop(0, w_in.shape[0] // BLOCK)
    def _(k):
        rows = pl.ds(pl.multiple_of(k * BLOCK, BLOCK), BLOCK)
        in_t[:, rows] = (
            jnp.dot(perm[...], w_in[rows, :], preferred_element_type=F32).astype(BF).T
        )

    done(in_t, in_t_hbm)
    copies[1].wait()

    @pl.loop(0, w_out.shape[1] // BLOCK)
    def _(k):
        rows = pl.ds(pl.multiple_of(k * BLOCK, BLOCK), BLOCK)
        out_t[rows, :] = jnp.dot(
            perm[...], w_out[:, rows].T, preferred_element_type=F32
        ).astype(BF)

    done(out_t, out_t_hbm)
    perm[...] = swap_rows(BLOCK, RADF)
    copies[2].wait()
    for k in range(w_rad.shape[0] // BLOCK):
        rows = slice(k * BLOCK, k * BLOCK + BLOCK)
        rad_t[:, rows] = (
            jnp.dot(perm[...], w_rad[rows, :], preferred_element_type=F32).astype(BF).T
        )
    done(rad_t, rad_t_hbm)
    copies[3].wait()
    heat_t[...] = w_heat[...].T
    done(heat_t, heat_t_hbm)
    for copy in results:
        copy.wait()


def gelu(x):
    return 0.5 * x * (1.0 + jnp.tanh(0.7978845608028654 * (x + 0.044715 * (x * x * x))))


def column_kernel(
    count, got, remap, in_hbm, out_hbm, rad_hbm, heat_hbm, day, back,
    whole, total, remapped, hidden, rad_in, rad_hidden, w_in, w_out, w_rad, w_heat, sems,
):
    copies = fetch(
        [(in_hbm, w_in), (out_hbm, w_out), (rad_hbm, w_rad), (heat_hbm, w_heat)], sems
    )
    ngroup, nf, nlev, ncol = got.shape
    levels = ngroup * nlev
    deep = BLOCK // nf
    w = remap[...]
    high = w.astype(BF)
    low = (w - high.astype(F32)).astype(BF)
    both = jnp.concatenate([high, low], axis=1)
    for two in range(nf // 2):
        ts = []
        for k in range(2):
            field = two * 2 + k
            code = got[:, field].astype(F32).reshape(levels, ncol)
            ts.append(jnp.log2(code) * (1.0 / SPREAD))
            whole[field * levels : field * levels + levels, :] = ts[-1]
        t = jnp.concatenate(ts, axis=1)
        th = t.astype(BF)
        tl = (t - th.astype(F32)).astype(BF)
        x = t + (
            jnp.dot(both, jnp.concatenate([th, th], axis=0), preferred_element_type=F32)
            + jnp.dot(high, tl, preferred_element_type=F32)
        )
        for k in range(2):
            for block in range(levels // deep):
                at = block * BLOCK + (two * 2 + k) * deep
                tile = x[block * deep : block * deep + deep, k * ncol : k * ncol + ncol]
                total[at : at + deep, :] = tile
                remapped[at : at + deep, :] = tile.astype(BF)
    copies[0].wait()
    for i in range(w_in.shape[0] // BLOCK):
        rows = slice(i * BLOCK, i * BLOCK + BLOCK)
        hidden[rows, :] = gelu(
            jnp.dot(w_in[rows, :], remapped[...], preferred_element_type=F32)
        ).astype(BF)
    copies[1].wait()
    blocks_each = levels // deep // (w_rad.shape[1] // BLOCK)
    for i in range(nf * levels // BLOCK):
        rows = slice(i * BLOCK, i * BLOCK + BLOCK)
        total[rows, :] = total[rows, :] + jnp.dot(
            w_out[rows, :], hidden[...], preferred_element_type=F32
        )
        for field in range(RADF):
            at = (i // blocks_each) * BLOCK + (field * blocks_each + i % blocks_each) * deep
            first = i * BLOCK + field * deep
            rad_in[at : at + deep, :] = total[first : first + deep, :].astype(BF)
    copies[2].wait()
    copies[3].wait()
    for i in range(w_rad.shape[0] // BLOCK):
        rows = slice(i * BLOCK, i * BLOCK + BLOCK)
        rad_hidden[rows, :] = gelu(
            jnp.dot(w_rad[rows, :], rad_in[...], preferred_element_type=F32)
        ).astype(BF)
    for field in range(1, nf):
        for group in range(ngroup):
            at = (group * nlev // deep) * BLOCK + field * deep + group * nlev % deep
            own = field * levels + group * nlev
            back[group, field] = (total[at : at + nlev, :] - whole[own : own + nlev, :]).astype(BF)
    warm = jnp.dot(w_heat[...], rad_hidden[...], preferred_element_type=F32)
    col = lax.broadcasted_iota(jnp.int32, (ncol, ncol), 0)
    rank = lax.broadcasted_iota(jnp.int32, (ncol, ncol), 1)
    hit = jnp.logical_and(day[...] == col, rank < count[0, 0] * DB)
    lit = lax.dot_general(
        jnp.ones((8, ncol), BF),
        jnp.where(hit, 1.0, 0.0).astype(BF),
        (((1,), (1,)), ((), ())),
        preferred_element_type=F32,
    )
    warm = jnp.where(jnp.broadcast_to(lit[:1, :], warm.shape) > 0.5, warm, 0.0)
    for group in range(ngroup):
        at = (group * nlev // deep) * BLOCK + group * nlev % deep
        own = group * nlev
        back[group, 0] = (
            total[at : at + nlev, :] - whole[own : own + nlev, :] + warm[own : own + nlev, :]
        ).astype(BF)


def finish_kernel(moved, change, out_hbm, turned, out, sems):
    nlev, nf, nrow, nlon = moved.shape
    copies = []
    for field in range(nf):
        for half in range(nlon // LANES):
            base = (field * 2 + half) * nrow * nlev
            for r in range(nrow):
                turned[pl.ds(base + r * nlev, nlev), :] = change[r * 2 + half, field].astype(F32)
            lanes = slice(half * LANES, half * LANES + LANES)
            for level in range(nlev):
                out[level, field, :, lanes] = (
                    moved[level, field, :, lanes]
                    + turned[pl.ds(base + level, nrow, stride=nlev), :]
                )
        if (field + 1) % SOME == 0:
            put = slice(field + 1 - SOME, field + 1)
            copies += fetch([(out.at[:, put], out_hbm.at[:, put])], sems.at[field // SOME])
    for copy in copies:
        copy.wait()


def on_device(
    state, cour_lat, cour_lev, cour_lon, remap_weight, w_in, w_out, w_rad_in,
    radiative_final_weights, day_list, day_count,
):
    nlev, nf, nrow, nlon = state.shape
    nlat_dev, nlev_dev = lax.axis_size("lat"), lax.axis_size("lev")
    levels = nlev * nlev_dev
    ncol = nrow * nlon // nlev_dev
    vmem = pl.BlockSpec(memory_space=pltpu.VMEM)
    hbm = pl.BlockSpec(memory_space=pltpu.HBM)
    shape = jax.ShapeDtypeStruct

    lat_rows, lev_rows = nlev * nf, nf * nrow
    packs = call(
        pack_kernel,
        "pack",
        (shape((lat_rows + nlev, nlon), BF),) * 2
        + (shape((lev_rows + nrow, nlon), BF),) * 2
        + (shape(state.shape, F32),)
        + (shape(cour_lat.shape, F32),) * 3,
        [hbm] * 4,
        [
            pltpu.VMEM((2, lat_rows, nlon), BF),
            pltpu.SemaphoreType.DMA((nlev + 3,)),
        ],
        moved=state.size * 4,
        limit=8 << 20,
    )(*map(in_hbm, (state, cour_lat, cour_lev, cour_lon)))
    packs, held = packs[:4], packs[4:]

    def trade(value, axis, count, first):
        pairs = [(i, i + 1) for i in range(first, count - 1, 2)]
        return lax.ppermute(value, axis, pairs + [(j, i) for i, j in pairs])

    halos = [
        trade(packs[0], "lat", nlat_dev, 0),
        trade(packs[1], "lat", nlat_dev, 1),
        trade(packs[2], "lev", nlev_dev, 0),
        trade(packs[3], "lev", nlev_dev, 1),
    ]
    part = call(
        interior_kernel,
        "interior",
        shape(state.shape, F32),
        [vmem] * 4,
        flops=state.size * 13,
        moved=state.size * 8,
        limit=8 << 20,
    )(*held)
    moved, sent = call(
        edge_kernel,
        "edges",
        (shape(state.shape, F32), pltpu.HBM((2 * nrow, nf, nlev, LANES), BF)),
        [vmem] * 9,
        [
            pltpu.VMEM((lat_rows, nlon), F32),
            pltpu.VMEM((lat_rows, nlon), F32),
            pltpu.VMEM((nf * 2 * nlev * nrow, LANES), F32),
            pltpu.VMEM((2 * nrow, nf, nlev, LANES), BF),
            pltpu.SemaphoreType.DMA((nf // SOME, 1)),
        ],
        limit=8 << 20,
        out_specs=(vmem, hbm),
    )(part, *packs, *halos)

    got = lax.all_to_all(sent, "lev", split_axis=0, concat_axis=0, tiled=True)

    nhid, nrad = w_in.shape[1], w_rad_in.shape[1]
    weights = (w_in, w_out, w_rad_in, radiative_final_weights)
    flipped = call(
        flip_kernel,
        "flip",
        tuple(pltpu.HBM(w.shape[::-1], BF) for w in weights),
        [hbm] * 4,
        [pltpu.VMEM(w.shape, BF) for w in weights]
        + [pltpu.VMEM(w.shape[::-1], BF) for w in weights]
        + [pltpu.VMEM((BLOCK, BLOCK), BF)]
        + [pltpu.SemaphoreType.DMA((4,))] * 2,
        flops=FLIP_FLOPS,
        moved=2 * sum(w.size * 2 for w in weights),
        limit=20 << 20,
        out_specs=(hbm,) * 4,
    )(*map(in_hbm, weights))
    back = call(
        column_kernel,
        "columns",
        shape(got.shape, BF),
        [pl.BlockSpec(memory_space=pltpu.SMEM)] + [vmem] * 2 + [hbm] * 4 + [vmem],
        [
            pltpu.VMEM((nf * levels, ncol), F32),
            pltpu.VMEM((nf * levels, ncol), F32),
            pltpu.VMEM((nf * levels, ncol), BF),
            pltpu.VMEM((nhid, ncol), BF),
            pltpu.VMEM((RADF * levels, ncol), BF),
            pltpu.VMEM((nrad, ncol), BF),
        ]
        + [pltpu.VMEM(w.shape[::-1], BF) for w in weights]
        + [pltpu.SemaphoreType.DMA((4,))],
        limit=20 << 20,
    )(day_count, got, remap_weight, *map(in_hbm, flipped), day_list.reshape(1, -1))

    change = lax.all_to_all(back, "lev", split_axis=0, concat_axis=0, tiled=True)
    return call(
        finish_kernel,
        "finish",
        pltpu.HBM(state.shape, F32),
        [vmem] * 2,
        [
            pltpu.VMEM((nf * 2 * nlev * nrow, LANES), F32),
            pltpu.VMEM(state.shape, F32),
            pltpu.SemaphoreType.DMA((nf // SOME, 1)),
        ],
        limit=8 << 20,
        out_specs=hbm,
    )(moved, change)


def solution(mesh):
    placed = (
        P("lev", None, "lat", None),
        P("lev", "lat", None),
        P("lev", "lat", None),
        P("lev", "lat", None),
        P(),
        P(),
        P(),
        P(),
        P(),
        P("lat", "lev", None),
        P("lat", "lev"),
    )
    return jax.shard_map(
        on_device,
        mesh=mesh,
        in_specs=placed,
        out_specs=P("lev", None, "lat", None),
        check_vma=False,
    )
```

```python
import jax
import jax.numpy as jnp
from jax import lax
from jax.experimental import pallas as pl
from jax.experimental.pallas import tpu as pltpu
from jax.sharding import PartitionSpec as P

RADF = 4
DB = 16
LANES = 128
BLOCK = 256
SOME = 4
BF = jnp.bfloat16
F32 = jnp.float32
VMEM_LIMIT = 16 << 20
FLIP_FLOPS = 4_000_000_000
SPREAD = 7.0


def call(
    kernel, name, out_shape, in_specs, scratch=(), flops=0, moved=0, limit=VMEM_LIMIT, out_specs=None
):
    vmem = pl.BlockSpec(memory_space=pltpu.VMEM)
    return pl.pallas_call(
        kernel,
        name=name,
        out_shape=out_shape,
        in_specs=in_specs,
        out_specs=out_specs or jax.tree.map(lambda _: vmem, out_shape),
        scratch_shapes=list(scratch),
        compiler_params=pltpu.CompilerParams(vmem_limit_bytes=limit),
        cost_estimate=pl.CostEstimate(flops=flops, bytes_accessed=moved, transcendentals=0),
    )


def in_hbm(array):
    return pltpu.with_memory_space_constraint(array, pltpu.HBM)


def fetch(pairs, sems):
    copies = [
        pltpu.make_async_copy(source, target, sems.at[i])
        for i, (source, target) in enumerate(pairs)
    ]
    for copy in copies:
        copy.start()
    return copies


def pack_kernel(
    state_hbm, lat_hbm, lev_hbm, lon_hbm, lat_pair, lat_other, lev_pair, lev_other,
    state, cour_lat, cour_lev, cour_lon, both, sems,
):
    nlev, nf, nrow, _ = state.shape
    order = [0, nlev - 1] + list(range(1, nlev - 1))
    copies = fetch(
        [(lev_hbm, cour_lev), (lat_hbm, cour_lat)]
        + [(state_hbm.at[level], state.at[level]) for level in order]
        + [(lon_hbm, cour_lon)],
        sems,
    )
    copies[0].wait()
    lev_pair[nf * nrow :, :] = cour_lev[nlev - 1].astype(BF)
    lev_other[nf * nrow :, :] = cour_lev[nlev - 1].astype(BF)
    copies[1].wait()
    rates = cour_lat[:, nrow - 1, :].astype(BF)
    lat_pair[nlev * nf :, :] = rates
    lat_other[nlev * nf :, :] = rates
    copies[2].wait()
    copies[3].wait()
    odd = lax.axis_index("lev") & 1
    lat_odd = lax.axis_index("lat") & 1
    for field in range(nf):
        rows = slice(field * nrow, field * nrow + nrow)
        lev_pair[rows, :] = state[(1 - odd) * (nlev - 1), field].astype(BF)
        lev_other[rows, :] = state[odd * (nlev - 1), field].astype(BF)
    for place, level in enumerate(order):
        if place > 1:
            copies[2 + place].wait()
        rows = slice(level * nf, level * nf + nf)
        block = state[level]
        both[0, rows, :] = block[:, nrow - 1, :].astype(BF)
        both[1, rows, :] = block[:, 0, :].astype(BF)
    lat_pair[: nlev * nf, :] = both[lat_odd]
    lat_other[: nlev * nf, :] = both[1 - lat_odd]
    copies[-1].wait()


def interior_kernel(state, cour_lat, cour_lev, cour_lon, part):
    nlev, nf, nrow, nlon = state.shape
    last_lat = lax.axis_index("lat") == lax.axis_size("lat") - 1
    last_lev = lax.axis_index("lev") == lax.axis_size("lev") - 1
    row = lax.broadcasted_iota(jnp.int32, (nrow, nlon), 0)
    first_row, last_row = row == 0, row == nrow - 1
    closed_lat = jnp.logical_and(last_row, last_lat)
    open_lev = jnp.where(last_lev, 0.0, 1.0).astype(F32)
    for level in range(nlev):
        n = jnp.where(closed_lat, 0.0, cour_lat[level])
        ns = jnp.where(first_row, 0.0, pltpu.roll(n, 1, 0))
        d = cour_lev[level] * open_lev if level == nlev - 1 else cour_lev[level]
        e = cour_lon[level]
        ew = pltpu.roll(e, 1, 1)
        mid = (
            1.0
            - (jnp.maximum(n, 0.0) - jnp.minimum(ns, 0.0))
            - (jnp.maximum(e, 0.0) - jnp.minimum(ew, 0.0))
            - jnp.maximum(d, 0.0)
        )
        c_n, c_s = jnp.where(last_row, 0.0, jnp.minimum(n, 0.0)), jnp.maximum(ns, 0.0)
        c_e, c_w = jnp.minimum(e, 0.0), jnp.maximum(ew, 0.0)
        c_d = jnp.minimum(d, 0.0)
        if level > 0:
            du = cour_lev[level - 1]
            mid = mid + jnp.minimum(du, 0.0)
            c_u = jnp.maximum(du, 0.0)
        for field in range(nf):
            q = state[level, field]
            t = (
                mid * q
                + (c_s * pltpu.roll(q, 1, 0) - c_n * pltpu.roll(q, nrow - 1, 0))
                + (c_w * pltpu.roll(q, 1, 1) - c_e * pltpu.roll(q, nlon - 1, 1))
            )
            if level > 0:
                t = t + c_u * state[level - 1, field]
            if level < nlev - 1:
                t = t - c_d * state[level + 1, field]
            part[level, field] = t


def edge_kernel(
    part, lat_pair, lat_other, lev_pair, lev_other,
    from_lat_pair, from_lat_other, from_lev_pair, from_lev_other,
    moved, sent_hbm, south, north, turned, sent, sems,
):
    nlev, nf, nrow, nlon = part.shape
    lat_odd, lev_odd = lax.axis_index("lat") & 1 == 1, lax.axis_index("lev") & 1 == 1

    def pick(odd, rows, if_odd, if_even):
        return jnp.where(odd, if_odd[rows, :].astype(F32), if_even[rows, :].astype(F32))

    tail = slice(nlev * nf, nlev * nf + nlev)
    south_rate = pick(lat_odd, tail, from_lat_pair, from_lat_other)
    north_rate = lat_pair[tail, :].astype(F32)
    for level in range(nlev):
        rows = slice(level * nf, level * nf + nf)
        rate = jnp.broadcast_to(south_rate[level : level + 1], (nf, nlon))
        south[rows, :] = jnp.minimum(rate, 0.0) * pick(
            lat_odd, rows, lat_pair, lat_other
        ) + jnp.maximum(rate, 0.0) * pick(lat_odd, rows, from_lat_pair, from_lat_other)
        rate = jnp.broadcast_to(north_rate[level : level + 1], (nf, nlon))
        north[rows, :] = -jnp.minimum(rate, 0.0) * pick(
            lat_odd, rows, from_lat_other, from_lat_pair
        )
    row = lax.broadcasted_iota(jnp.int32, (nrow, nlon), 0)
    first_row, last_row = row == 0, row == nrow - 1
    tail = slice(nf * nrow, nf * nrow + nrow)
    above_rate = pick(lev_odd, tail, from_lev_pair, from_lev_other)
    below_rate = lev_pair[tail, :].astype(F32)
    u_in, u_out = jnp.maximum(above_rate, 0.0), jnp.minimum(above_rate, 0.0)
    d_in = jnp.minimum(below_rate, 0.0)
    copies = []
    for field in range(nf):
        for level in range(nlev):
            at = level * nf + field
            t = part[level, field] + jnp.where(
                first_row,
                jnp.broadcast_to(south[at : at + 1, :], (nrow, nlon)),
                jnp.where(last_row, jnp.broadcast_to(north[at : at + 1, :], (nrow, nlon)), 0.0),
            )
            rows = slice(field * nrow, field * nrow + nrow)
            if level == 0:
                t = (
                    t
                    + u_out * pick(lev_odd, rows, lev_pair, lev_other)
                    + u_in * pick(lev_odd, rows, from_lev_pair, from_lev_other)
                )
            if level == nlev - 1:
                t = t - d_in * pick(lev_odd, rows, from_lev_other, from_lev_pair)
            moved[level, field] = t
            for half in range(nlon // LANES):
                turned[pl.ds(((field * 2 + half) * nlev + level) * nrow, nrow), :] = t[
                    :, half * LANES : half * LANES + LANES
                ]
        for half in range(nlon // LANES):
            for r in range(nrow):
                tile = turned[pl.ds((field * 2 + half) * nlev * nrow + r, nlev, stride=nrow), :]
                sent[r * 2 + half, field] = jnp.exp2(tile * SPREAD).astype(BF)
        if (field + 1) % SOME == 0:
            put = slice(field + 1 - SOME, field + 1)
            copies += fetch([(sent.at[:, put], sent_hbm.at[:, put])], sems.at[field // SOME])
    for copy in copies:
        copy.wait()


def swap_rows(rows, inner):
    to = lax.broadcasted_iota(jnp.int32, (rows, rows), 0)
    source = lax.broadcasted_iota(jnp.int32, (rows, rows), 1)
    outer = rows // inner
    wanted = lax.rem(to, outer) * inner + lax.div(to, outer)
    return jnp.where(source == wanted, 1.0, 0.0).astype(BF)


def flip_kernel(
    in_hbm, out_hbm, rad_hbm, heat_hbm, in_t_hbm, out_t_hbm, rad_t_hbm, heat_t_hbm,
    w_in, w_out, w_rad, w_heat, in_t, out_t, rad_t, heat_t, perm, sems, out_sems,
):
    copies = fetch([(in_hbm, w_in), (out_hbm, w_out), (rad_hbm, w_rad), (heat_hbm, w_heat)], sems)
    perm[...] = swap_rows(BLOCK, BLOCK // 16)
    results = []

    def done(source, target):
        results.append(pltpu.make_async_copy(source, target, out_sems.at[len(results)]))
        results[-1].start()

    copies[0].wait()

    @pl.loop(0, w_in.shape[0] // BLOCK)
    def _(k):
        rows = pl.ds(pl.multiple_of(k * BLOCK, BLOCK), BLOCK)
        in_t[:, rows] = (
            jnp.dot(perm[...], w_in[rows, :], preferred_element_type=F32).astype(BF).T
        )

    done(in_t, in_t_hbm)
    copies[1].wait()

    @pl.loop(0, w_out.shape[1] // BLOCK)
    def _(k):
        rows = pl.ds(pl.multiple_of(k * BLOCK, BLOCK), BLOCK)
        out_t[rows, :] = jnp.dot(
            perm[...], w_out[:, rows].T, preferred_element_type=F32
        ).astype(BF)

    done(out_t, out_t_hbm)
    perm[...] = swap_rows(BLOCK, RADF)
    copies[2].wait()
    for k in range(w_rad.shape[0] // BLOCK):
        rows = slice(k * BLOCK, k * BLOCK + BLOCK)
        rad_t[:, rows] = (
            jnp.dot(perm[...], w_rad[rows, :], preferred_element_type=F32).astype(BF).T
        )
    done(rad_t, rad_t_hbm)
    copies[3].wait()
    heat_t[...] = w_heat[...].T
    done(heat_t, heat_t_hbm)
    for copy in results:
        copy.wait()


def gelu(x):
    return 0.5 * x * (1.0 + jnp.tanh(0.7978845608028654 * (x + 0.044715 * (x * x * x))))


def column_kernel(
    count, got, remap, in_hbm, out_hbm, rad_hbm, heat_hbm, day, back,
    whole, total, remapped, hidden, rad_in, rad_hidden, w_in, w_out, w_rad, w_heat, sems,
):
    pieces = []
    for source, target in ((in_hbm, w_in), (out_hbm, w_out), (rad_hbm, w_rad)):
        for at in range(0, source.shape[0], BLOCK):
            pieces.append((source.at[at : at + BLOCK], target.at[at : at + BLOCK]))
    copies = iter(fetch(pieces + [(heat_hbm, w_heat)], sems))
    ngroup, nf, nlev, ncol = got.shape
    levels = ngroup * nlev
    deep = BLOCK // nf
    w = remap[...]
    high = w.astype(BF)
    low = (w - high.astype(F32)).astype(BF)
    both = jnp.concatenate([high, low], axis=1)
    for two in range(nf // 2):
        ts = []
        for k in range(2):
            field = two * 2 + k
            code = got[:, field].astype(F32).reshape(levels, ncol)
            ts.append(jnp.log2(code) * (1.0 / SPREAD))
            whole[field * levels : field * levels + levels, :] = ts[-1]
        t = jnp.concatenate(ts, axis=1)
        th = t.astype(BF)
        tl = (t - th.astype(F32)).astype(BF)
        x = t + (
            jnp.dot(both, jnp.concatenate([th, th], axis=0), preferred_element_type=F32)
            + jnp.dot(high, tl, preferred_element_type=F32)
        )
        for k in range(2):
            for block in range(levels // deep):
                at = block * BLOCK + (two * 2 + k) * deep
                tile = x[block * deep : block * deep + deep, k * ncol : k * ncol + ncol]
                total[at : at + deep, :] = tile
                remapped[at : at + deep, :] = tile.astype(BF)
    for i in range(w_in.shape[0] // BLOCK):
        next(copies).wait()
        rows = slice(i * BLOCK, i * BLOCK + BLOCK)
        hidden[rows, :] = gelu(
            jnp.dot(w_in[rows, :], remapped[...], preferred_element_type=F32)
        ).astype(BF)
    blocks_each = levels // deep // (w_rad.shape[1] // BLOCK)
    for i in range(nf * levels // BLOCK):
        next(copies).wait()
        rows = slice(i * BLOCK, i * BLOCK + BLOCK)
        total[rows, :] = total[rows, :] + jnp.dot(
            w_out[rows, :], hidden[...], preferred_element_type=F32
        )
        for field in range(RADF):
            at = (i // blocks_each) * BLOCK + (field * blocks_each + i % blocks_each) * deep
            first = i * BLOCK + field * deep
            rad_in[at : at + deep, :] = total[first : first + deep, :].astype(BF)
    for i in range(w_rad.shape[0] // BLOCK):
        next(copies).wait()
        rows = slice(i * BLOCK, i * BLOCK + BLOCK)
        rad_hidden[rows, :] = gelu(
            jnp.dot(w_rad[rows, :], rad_in[...], preferred_element_type=F32)
        ).astype(BF)
    for field in range(1, nf):
        for group in range(ngroup):
            at = (group * nlev // deep) * BLOCK + field * deep + group * nlev % deep
            own = field * levels + group * nlev
            back[group, field] = (total[at : at + nlev, :] - whole[own : own + nlev, :]).astype(BF)
    next(copies).wait()
    warm = jnp.dot(w_heat[...], rad_hidden[...], preferred_element_type=F32)
    col = lax.broadcasted_iota(jnp.int32, (ncol, ncol), 0)
    rank = lax.broadcasted_iota(jnp.int32, (ncol, ncol), 1)
    hit = jnp.logical_and(day[...] == col, rank < count[0, 0] * DB)
    lit = lax.dot_general(
        jnp.ones((8, ncol), BF),
        jnp.where(hit, 1.0, 0.0).astype(BF),
        (((1,), (1,)), ((), ())),
        preferred_element_type=F32,
    )
    warm = jnp.where(jnp.broadcast_to(lit[:1, :], warm.shape) > 0.5, warm, 0.0)
    for group in range(ngroup):
        at = (group * nlev // deep) * BLOCK + group * nlev % deep
        own = group * nlev
        back[group, 0] = (
            total[at : at + nlev, :] - whole[own : own + nlev, :] + warm[own : own + nlev, :]
        ).astype(BF)


def finish_kernel(moved, change, out_hbm, turned, out, sems):
    nlev, nf, nrow, nlon = moved.shape
    copies = []
    for field in range(nf):
        for half in range(nlon // LANES):
            base = (field * 2 + half) * nrow * nlev
            for r in range(nrow):
                turned[pl.ds(base + r * nlev, nlev), :] = change[r * 2 + half, field].astype(F32)
            lanes = slice(half * LANES, half * LANES + LANES)
            for level in range(nlev):
                out[level, field, :, lanes] = (
                    moved[level, field, :, lanes]
                    + turned[pl.ds(base + level, nrow, stride=nlev), :]
                )
        if (field + 1) % SOME == 0:
            put = slice(field + 1 - SOME, field + 1)
            copies += fetch([(out.at[:, put], out_hbm.at[:, put])], sems.at[field // SOME])
    for copy in copies:
        copy.wait()


def on_device(
    state, cour_lat, cour_lev, cour_lon, remap_weight, w_in, w_out, w_rad_in,
    radiative_final_weights, day_list, day_count,
):
    nlev, nf, nrow, nlon = state.shape
    nlat_dev, nlev_dev = lax.axis_size("lat"), lax.axis_size("lev")
    levels = nlev * nlev_dev
    ncol = nrow * nlon // nlev_dev
    vmem = pl.BlockSpec(memory_space=pltpu.VMEM)
    hbm = pl.BlockSpec(memory_space=pltpu.HBM)
    shape = jax.ShapeDtypeStruct

    lat_rows, lev_rows = nlev * nf, nf * nrow
    packs = call(
        pack_kernel,
        "pack",
        (shape((lat_rows + nlev, nlon), BF),) * 2
        + (shape((lev_rows + nrow, nlon), BF),) * 2
        + (shape(state.shape, F32),)
        + (shape(cour_lat.shape, F32),) * 3,
        [hbm] * 4,
        [
            pltpu.VMEM((2, lat_rows, nlon), BF),
            pltpu.SemaphoreType.DMA((nlev + 3,)),
        ],
        moved=state.size * 4,
        limit=8 << 20,
    )(*map(in_hbm, (state, cour_lat, cour_lev, cour_lon)))
    packs, held = packs[:4], packs[4:]

    def trade(value, axis, count, first):
        pairs = [(i, i + 1) for i in range(first, count - 1, 2)]
        return lax.ppermute(value, axis, pairs + [(j, i) for i, j in pairs])

    halos = [
        trade(packs[0], "lat", nlat_dev, 0),
        trade(packs[1], "lat", nlat_dev, 1),
        trade(packs[2], "lev", nlev_dev, 0),
        trade(packs[3], "lev", nlev_dev, 1),
    ]
    part = call(
        interior_kernel,
        "interior",
        shape(state.shape, F32),
        [vmem] * 4,
        flops=state.size * 13,
        moved=state.size * 8,
        limit=8 << 20,
    )(*held)
    moved, sent = call(
        edge_kernel,
        "edges",
        (shape(state.shape, F32), pltpu.HBM((2 * nrow, nf, nlev, LANES), BF)),
        [vmem] * 9,
        [
            pltpu.VMEM((lat_rows, nlon), F32),
            pltpu.VMEM((lat_rows, nlon), F32),
            pltpu.VMEM((nf * 2 * nlev * nrow, LANES), F32),
            pltpu.VMEM((2 * nrow, nf, nlev, LANES), BF),
            pltpu.SemaphoreType.DMA((nf // SOME, 1)),
        ],
        limit=8 << 20,
        out_specs=(vmem, hbm),
    )(part, *packs, *halos)

    got = lax.all_to_all(sent, "lev", split_axis=0, concat_axis=0, tiled=True)

    nhid, nrad = w_in.shape[1], w_rad_in.shape[1]
    weights = (w_in, w_out, w_rad_in, radiative_final_weights)
    flipped = call(
        flip_kernel,
        "flip",
        tuple(pltpu.HBM(w.shape[::-1], BF) for w in weights),
        [hbm] * 4,
        [pltpu.VMEM(w.shape, BF) for w in weights]
        + [pltpu.VMEM(w.shape[::-1], BF) for w in weights]
        + [pltpu.VMEM((BLOCK, BLOCK), BF)]
        + [pltpu.SemaphoreType.DMA((4,))] * 2,
        flops=FLIP_FLOPS,
        moved=2 * sum(w.size * 2 for w in weights),
        limit=20 << 20,
        out_specs=(hbm,) * 4,
    )(*map(in_hbm, weights))
    back = call(
        column_kernel,
        "columns",
        shape(got.shape, BF),
        [pl.BlockSpec(memory_space=pltpu.SMEM)] + [vmem] * 2 + [hbm] * 4 + [vmem],
        [
            pltpu.VMEM((nf * levels, ncol), F32),
            pltpu.VMEM((nf * levels, ncol), F32),
            pltpu.VMEM((nf * levels, ncol), BF),
            pltpu.VMEM((nhid, ncol), BF),
            pltpu.VMEM((RADF * levels, ncol), BF),
            pltpu.VMEM((nrad, ncol), BF),
        ]
        + [pltpu.VMEM(w.shape[::-1], BF) for w in weights]
        + [pltpu.SemaphoreType.DMA(((nhid + nf * levels + nrad) // BLOCK + 1,))],
        limit=20 << 20,
    )(day_count, got, remap_weight, *map(in_hbm, flipped), day_list.reshape(1, -1))

    change = lax.all_to_all(back, "lev", split_axis=0, concat_axis=0, tiled=True)
    return call(
        finish_kernel,
        "finish",
        pltpu.HBM(state.shape, F32),
        [vmem] * 2,
        [
            pltpu.VMEM((nf * 2 * nlev * nrow, LANES), F32),
            pltpu.VMEM(state.shape, F32),
            pltpu.SemaphoreType.DMA((nf // SOME, 1)),
        ],
        limit=8 << 20,
        out_specs=hbm,
    )(moved, change)


def solution(mesh):
    placed = (
        P("lev", None, "lat", None),
        P("lev", "lat", None),
        P("lev", "lat", None),
        P("lev", "lat", None),
        P(),
        P(),
        P(),
        P(),
        P(),
        P("lat", "lev", None),
        P("lat", "lev"),
    )
    return jax.shard_map(
        on_device,
        mesh=mesh,
        in_specs=placed,
        out_specs=P("lev", None, "lat", None),
        check_vma=False,
    )
```
